512 devices in a mesh: grp: 2 (over core), mer: 64 (over y, z), sub: 4 (over x).
Axes of the slice: x: 4, y: 8, z: 8, core: 2. Of those that a mesh axis runs over, the one named last changes fastest.
Arguments:
- field: float32 [2, 256, 262144], P('grp', 'sub', 'mer'), may hold values from -6 to 6
- previous: float32 [2, 256, 262144], P('grp', 'sub', 'mer'), may hold values from -6 to 6
- stiff: float32 [2, 128, 128], P('grp'), as said below
- synth: float32 [2, 256, 256], P('grp', None, 'sub'), may hold values from -0.5 to 0.5
- owner: int32 [2, 16384, 1], P('grp', 'mer'), may hold values from 0 to 63; in each aligned block of 256 rows (0 to 255, 256 to 511, ..., all dimensions but the last counted through in order) at most 8 rows name the same one
- face: int32 [2, 16384], P('grp', 'mer'), may hold values from 0 to 255
- weight: float32 [2, 16384], P('grp', 'mer'), may hold values from 0.3 to 1.7
Outputs:
- latest: float32 [2, 256, 262144], P('grp', 'sub', 'mer')
- prior: float32 [2, 256, 262144], P('grp', 'sub', 'mer')
The draws below stay inside these ranges and needn't reach their ends.
Inputs may be any that keep to these rules, and one draw needn't show every extreme that they name: Among the 256 interface points of one domain, at most 8 name the same owner, and in some domains exactly 8 do. `stiff`: each model's element matrix is symmetric.
All inputs are finite; a program needn't handle non-finite values.
Results may differ from the reference program's by a relative error of at most 0.0001.
Values sent between devices are 32-bit elements; how exact they have to be, the bound alone decides.
A program may use at most 64 MiB of HBM per device.

```python
import math
import jax
import jax.numpy as jnp
import numpy as np
from jax import lax

CH = 256
PTS = 4096
EP = 128
IFC = 256
ITERS = 2
POINTS = 262144
CAP = 8
N_MER = 64


def draw_stiff(key, part):
    random_part = jax.random.normal(key, (2, EP, EP), jnp.float32)
    random_part = random_part * (0.25 / EP ** 0.5)
    symmetric = (random_part + jnp.swapaxes(random_part, 1, 2)) / 2.0 ** 0.5
    return (jnp.eye(EP, dtype=jnp.float32)[None, :, :] + symmetric).astype(jnp.float32)


def touch_ends(values, own_key, low, top_value):
    place = [jax.random.randint(jax.random.fold_in(own_key, axis), (), 0, length) for axis, length in enumerate(values.shape)]
    longest = values.shape.index(max(values.shape))
    neighbour = place[:longest] + [(place[longest] + 1) % values.shape[longest]] + place[longest + 1:]
    return values.at[tuple(place)].set(low).at[tuple(neighbour)].set(top_value)


def with_spikes(drawn, key, source, target, parts, factor):
    owner, partner = [(jnp.arange(drawn.shape[position]) // (drawn.shape[position] // parts)).reshape([-1 if axis == position else 1 for axis in range(drawn.ndim)]) for position in (source, target)]
    chosen = jax.random.permutation(key, parts)[partner]
    strong = (owner == chosen) | (owner == (partner + parts // 2) % parts)
    return jnp.where(strong, factor * drawn, drawn)


def level_of(own_key, shape, cuts, low, top_value):
    level = 1.0
    for axis_at, parts in cuts:
        steps = jax.random.uniform(jax.random.fold_in(jax.random.fold_in(own_key, 6), axis_at), (parts,), jnp.float32, low / len(cuts), top_value / len(cuts))
        level = level * jnp.repeat(jnp.exp(steps), shape[axis_at] // parts).reshape((-1,) + (1,) * (len(shape) - 1 - axis_at))
    return level


def deal_out(rng, own, number, rows, number_of, top, reach, lean):
    order = jax.random.permutation(rng, number_of)
    crowded, ordinary = portions_of(number_of, rows * top, reach, lean, True), portions_of(number_of, rows * top, reach, lean, False)
    places = jnp.arange(number_of)

    def named(sizes, rotation):
        used = int((sizes > 0).sum())
        fixed = max(1, used // 4)
        moved = fixed + (places - fixed + rotation * (used - fixed)) % max(1, number_of - fixed)
        return jnp.zeros((number_of,), jnp.int32).at[order[jnp.where(places < fixed, places, moved)]].set(jnp.asarray(sizes, jnp.int32))

    sizes = jnp.where(number % 4 == 0, named(crowded, number // 4), named(ordinary, number - number // 4 - 1))
    mixed = jax.random.permutation(jax.random.fold_in(own, 3), number_of)
    source_of, taker = mixed[0:number_of // 2 * 2:2], mixed[1:number_of // 2 * 2:2]
    slack = jnp.minimum(sizes[source_of] - 1, reach - sizes[taker]) // 2
    slack = jnp.where((source_of == order[0]) | (taker == order[0]) | (sizes[taker] == 0), 0, jnp.maximum(slack, 0))
    moved = jax.random.randint(jax.random.fold_in(own, 4), (number_of // 2,), 0, 1 << 20) % (slack + 1)
    sizes = sizes.at[source_of].add(-moved).at[taker].add(moved)
    items = jnp.searchsorted(jnp.cumsum(sizes), jnp.arange(rows * top), side="right").astype(jnp.int32)
    grid = items.reshape(top, rows).T
    grid = grid[jax.random.permutation(jax.random.fold_in(own, 1), rows)]
    rotation = jax.random.randint(jax.random.fold_in(own, 2), (rows, 1), 0, top)
    return jnp.take_along_axis(grid, (jnp.arange(top)[None, :] + rotation) % top, axis=1)


def portions_of(number_of, total, most, lean, full):
    weights = [(1 << 20) // math.isqrt(grade ** lean) + 1 for grade in range(1, number_of + 1)]
    largest = most if full else min(most, max(-(-total // number_of), total * weights[0] // sum(weights)))
    least = 1 if total - largest >= number_of - 1 else 0
    counts, spare = [largest] + [least] * (number_of - 1), total - largest - least * (number_of - 1)
    while spare > 0:
        candidates = [i for i in range(1, number_of) if counts[i] < largest] or [i for i in range(1, number_of) if counts[i] < most]
        whole, left = sum([weights[i] for i in candidates]), spare
        for i in candidates:
            addition = min(most - counts[i], max(1, left * weights[i] // whole), spare)
            counts[i] = counts[i] + addition
            spare = spare - addition
    return np.array(counts)


def gaussian(rng, shape, spread, most, cuts=(), kind=jnp.bfloat16):
    loudness = level_of(rng, shape, cuts, -0.22, 0.18) if cuts else 1.0
    entries = jax.random.normal(rng, shape, jnp.float32) * spread * loudness
    return jnp.minimum(jnp.maximum(entries, -most), most).astype(kind)


def gaussian_with(stream_key, extent, width, limit, split, heavy, kind=jnp.bfloat16):
    drawn = width * jax.random.normal(stream_key, extent, jnp.float32)
    if split:
        drawn = drawn * level_of(stream_key, extent, split, -0.22, 0.18)
    return jnp.clip(with_spikes(drawn, jax.random.fold_in(stream_key, 3), *heavy), -limit, limit).astype(kind)


def setup_inputs(seed: int = 0) -> dict:
    key_list = jax.random.split(jax.random.key(seed), 8)
    field = gaussian(key_list[0], (2, CH, POINTS), 1.0, 6.0, ((0, 2), (1, 4), (2, 64)), jnp.float32)
    previous = gaussian(key_list[1], (2, CH, POINTS), 1.0, 6.0, ((0, 2), (1, 4), (2, 64)), jnp.float32)
    stiff = draw_stiff(jax.random.fold_in(key_list[7], 71), 0)
    synth = gaussian_with(key_list[3], (2, CH, CH), CH ** -0.5, 0.5, ((0, 2), (2, 4)), (2, 1, 4, 2.0), jnp.float32)
    owner_keys = jax.random.split(jax.random.fold_in(key_list[4], 1), 2 * (POINTS * IFC // PTS) // IFC)
    owner_turns = jax.random.permutation(jax.random.fold_in(key_list[4], 3), 2 * (POINTS * IFC // PTS) // IFC)
    owner = jax.vmap(lambda own, number: deal_out(jax.random.fold_in(key_list[4], 2), own, number, IFC, N_MER, 1, CAP, 2))(owner_keys, owner_turns).reshape((2, POINTS * IFC // PTS, 1))
    face = touch_ends(jax.random.randint(key_list[5], (2, POINTS * IFC // PTS), 0, IFC), jax.random.fold_in(key_list[5], 1), 0, IFC - 1).astype(jnp.int32)
    weight = jnp.clip(0.3 + 1.40000004 * jax.random.uniform(key_list[6], (2, POINTS * IFC // PTS), jnp.float32) ** level_of(key_list[6], (2, POINTS * IFC // PTS), ((0, 2), (1, 64)), -0.2, 0.2), 0.3, 1.7)
    return dict(field=field, previous=previous, stiff=stiff, synth=synth, owner=owner, face=face, weight=weight)


DT2 = 0.5
KAPPA = 0.5


def advance(state, older, stiff, synth, owner, face, weight):
    total = state.shape[2]
    padded = jnp.pad(state, ((0, 0), (0, 0), (1, 1)))
    lap = 2.0 * state - padded[:, :, 2:] - padded[:, :, :-2]
    blocks = state.reshape(2, CH, total // EP, EP)
    stiffened = jnp.einsum("gcne,gef->gcnf", blocks, stiff, precision=lax.Precision.HIGHEST).reshape(state.shape)
    shards = state.reshape(2, CH, N_MER, PTS)
    surface = shards[:, :, :, :IFC].reshape(2, CH, N_MER * IFC)
    traces = jnp.einsum("goc,gci->goi", synth, surface, precision=lax.Precision.HIGHEST) * weight[:, None, :]
    forces = []
    for group in range(2):
        target = (owner[group, :, 0] * IFC + face[group]).astype(jnp.int32)
        summed = jax.ops.segment_sum(traces[group].T, target, num_segments=N_MER * IFC)
        forces.append(summed.T)
    incoming = jnp.stack([forces[1], forces[0]]).reshape(2, CH, N_MER, IFC)
    forcing = jnp.pad(incoming, ((0, 0), (0, 0), (0, 0), (0, PTS - IFC))).reshape(state.shape)
    newer = 2.0 * state - older + DT2 * (forcing - stiffened - KAPPA * lap)
    return newer, state


def reference(field, previous, stiff, synth, owner, face, weight):
    state, older = field, previous
    for step in range(ITERS):
        state, older = advance(state, older, stiff, synth, owner, face, weight)
    return state, older
```

```python
import functools
import math

import jax
import jax.numpy as jnp
from jax import lax
from jax.experimental import pallas as pl
from jax.experimental.pallas import tpu as pltpu
from jax.sharding import PartitionSpec as P

MESH = pl.DeviceIdType.MESH
F32, BF16 = jnp.float32, jnp.bfloat16
LANES = 128
NT = (((1,), (1,)), ((), ()))


def halves(value):
    high = value.astype(BF16)
    return high, (value - high.astype(F32)).astype(BF16)


def iota(shape, dim):
    return lax.broadcasted_iota(jnp.int32, shape, dim).astype(F32)


def lanes_at(n, count):
    start = n * LANES
    return pl.ds(start if isinstance(n, int) else pl.multiple_of(start, LANES), count * LANES)


def dot(a, b):
    return jnp.dot(a, b, preferred_element_type=F32)


def kernel(
    ny, nz, nsub, field, previous, stiff, synth_t, owner, face, weight, latest, prior,
    state, older, newer, final, stiff_v, synth_v, owner_v, face_v, weight_v,
    part, part_in, packed, arrived, labels, labels_in,
    element, operator, pick, place, base,
    load_sem, part_send, part_recv, pack_send, pack_recv, halo_send, halo_recv, near_sem, out_sem,
):
    rows, points = older.shape
    tiles = points // LANES
    domains, height, _ = labels.shape
    iface = domains * height
    itiles = iface // LANES
    grp, mer, sub = lax.axis_index("grp"), lax.axis_index("mer"), lax.axis_index("sub")
    other = 1 - grp
    y, z = mer // nz, mer % nz
    above, below = (mer + 1) % domains, (mer + domains - 1) % domains

    barrier = pltpu.get_barrier_semaphore()

    def greet(sem, **where):
        pl.semaphore_signal(sem, inc=1, device_id=where, device_id_type=MESH)

    for k in range(1, nsub):
        greet(barrier, grp=grp, mer=mer, sub=(sub + k) % nsub)
    for k in range(1, nz):
        greet(barrier, grp=grp, mer=y * nz + (z + k) % nz, sub=sub)
    for k in range(ny):
        greet(barrier, grp=other, mer=(y + k) % ny * nz + z, sub=sub)
    greet(barrier, grp=grp, mer=above, sub=sub)
    greet(barrier, grp=grp, mer=below, sub=sub)

    def load(src, dst, n):
        copy = pltpu.make_async_copy(src, dst, load_sem.at[n])
        copy.start()
        return copy

    get_synth = load(synth_t.at[0], synth_v, 0)
    get_iface = load(field.at[0, :, pl.ds(0, iface)], state.at[:, pl.ds(LANES, iface)], 1)
    get_owner = load(owner, owner_v, 2)
    get_face = load(face, face_v, 3)
    get_weight = load(weight, weight_v, 4)
    get_stiff = load(stiff.at[0], stiff_v, 5)
    get_state = load(
        field.at[0, :, pl.ds(iface, points - iface)], state.at[:, pl.ds(LANES + iface, points - iface)], 6
    )
    get_older = load(previous.at[0], older, 7)

    def traces(value, step):
        high, low = halves(value)
        sums = dot(operator[...], jnp.concatenate([high, low, high, low], axis=0))
        part[step] = sums.reshape(nsub, rows, iface)

    def part_copy(step, k):
        to = (sub + k) % nsub
        return pltpu.make_async_remote_copy(
            src_ref=part.at[step, to],
            dst_ref=part_in.at[step, k - 1],
            send_sem=part_send.at[step, k - 1],
            recv_sem=part_recv.at[step, k - 1],
            device_id={"grp": grp, "mer": mer, "sub": to},
            device_id_type=MESH,
        )

    ways = sorted(range(1, nsub), key=lambda k: -min(k, nsub - k))

    get_synth.wait()
    high, low = halves(synth_v[...])
    high, low = high.astype(F32), low.astype(F32)
    operator[...] = jnp.concatenate([high, high, low, low], axis=0).T.astype(BF16)
    get_iface.wait()
    traces(state[:, LANES : LANES + iface], 0)

    pl.semaphore_wait(barrier, nsub - 1 + nz - 1 + ny + 2)
    for k in ways:
        part_copy(0, k).start()
    for k in range(ny):
        greet(near_sem, grp=other, mer=(y + k) % ny * nz + z, sub=sub)

    def halo_copy(src, dst, to, step, way):
        return pltpu.make_async_remote_copy(
            src_ref=src,
            dst_ref=dst,
            send_sem=halo_send.at[step, way],
            recv_sem=halo_recv.at[step, way],
            device_id={"grp": grp, "mer": to, "sub": sub},
            device_id_type=MESH,
        )

    def tile(ref, n, count=1):
        return ref.at[:, pl.ds(n * LANES, count * LANES)]

    up = [
        halo_copy(field.at[0, :, pl.ds(points - LANES, LANES)], tile(state, 0), above, 0, 0),
        halo_copy(tile(newer, tiles), tile(newer, 0), above, 1, 0),
    ]
    down = [
        halo_copy(field.at[0, :, pl.ds(0, LANES)], tile(state, tiles + 1), below, 0, 1),
        halo_copy(tile(newer, 1), tile(newer, tiles + 1), below, 1, 1),
    ]
    up[0].start()
    down[0].start()

    get_owner.wait()
    get_face.wait()
    get_weight.wait()
    own = owner_v[...].astype(F32)
    across = jnp.broadcast_to(own, (iface, iface))
    i, j = iota((iface, iface), 0), iota((iface, iface), 1)
    down_own = jnp.sum(jnp.where(i == j, across, 0.0), axis=1, keepdims=True)
    rank = jnp.sum(jnp.where((down_own == across) & (i < j), 1.0, 0.0), axis=0, keepdims=True)
    second = (rank >= height).astype(F32)
    row = own * height + rank - height * second
    hit = jnp.where(i == row, 1.0, 0.0)
    pick[0:iface, :] = (hit * (1.0 - second)).astype(BF16)
    pick[iface:, :] = (hit * second).astype(BF16)
    left_half = lax.broadcasted_iota(jnp.int32, (iface, LANES), 1) < LANES // 2
    names = jnp.broadcast_to(face_v[...].astype(F32), (LANES, iface)).astype(BF16)
    named = lax.dot_general(pick[...], names, NT, preferred_element_type=F32)
    labels[...] = jnp.where(left_half, named[:iface], named[iface:]).reshape(labels.shape)

    def owner_copy(src, dst, n, k):
        to = (y + ny // 2 + k // nz) % ny * nz + (z + nz // 2 + k % nz) % nz
        return pltpu.make_async_remote_copy(
            src_ref=src.at[to],
            dst_ref=dst.at[mer],
            send_sem=pack_send.at[n],
            recv_sem=pack_recv.at[n],
            device_id={"grp": other, "mer": to, "sub": sub},
            device_id_type=MESH,
        )

    def send_all(src, dst, n):
        def one(k, carry):
            owner_copy(src, dst, n, k).start()
            return carry

        lax.fori_loop(0, domains, one, 0, unroll=8)

    def all_of(src, dst, n):
        return pltpu.make_async_remote_copy(
            src_ref=src,
            dst_ref=dst,
            send_sem=pack_send.at[n],
            recv_sem=pack_recv.at[n],
            device_id={"grp": other, "mer": mer, "sub": sub},
            device_id_type=MESH,
        )

    pl.semaphore_wait(near_sem, ny)
    send_all(labels, labels_in, ITERS)

    def exchange(step):
        total = part[step, sub]
        for k in ways[::-1]:
            part_copy(step, k).wait_recv()
            total = total + part_in[step, k - 1]
        total = total * weight_v[...]
        high, low = halves(total)
        both = jnp.concatenate([high, low], axis=0)
        out = lax.dot_general(pick[...], both, NT, preferred_element_type=F32)
        out = out + pltpu.roll(out, LANES // 2, 1)
        packed[step] = jnp.where(left_half, out[:iface], out[iface:]).reshape(labels.shape)
        send_all(packed.at[step], arrived.at[step], step)

    exchange(0)

    get_stiff.wait()
    high, low = halves(stiff_v[...] * DT2)
    both = jnp.concatenate([high, low], axis=1)
    element[...] = jnp.concatenate([both, both], axis=0)
    lane = lax.broadcasted_iota(jnp.int32, (rows, LANES), 1)
    inner_low = jnp.where(mer > 0, 1.0, 0.0)
    inner_high = jnp.where(mer < domains - 1, 1.0, 0.0)

    def stepped(now, before, n, count, first=False, last=False):
        chunk = now[:, lanes_at(n, count + 2)]
        old = before(n, count)
        x = [chunk[:, LANES * c : LANES * (c + 1)] for c in range(count + 2)]
        if first:
            x[0] = x[0] * inner_low
        if last:
            x[-1] = x[-1] * inner_high
        high, low = halves(jnp.concatenate(x[1:-1], axis=0))
        product = dot(jnp.concatenate([high, low], axis=1), element[...])
        product = product[:, :LANES] + product[:, LANES:]
        right = [pltpu.roll(v, 1, 1) for v in x[:-1]]
        left = [pltpu.roll(v, LANES - 1, 1) for v in x[1:]]
        out = []
        for c in range(count):
            lower = jnp.where(lane == 0, right[c], right[c + 1])
            upper = jnp.where(lane == LANES - 1, left[c + 1], left[c])
            v = x[c + 1]
            lap = 2.0 * v - lower - upper
            out.append(
                2.0 * v - old[:, LANES * c : LANES * (c + 1)]
                - product[rows * c : rows * (c + 1)] - (DT2 * KAPPA) * lap
            )
        return jnp.concatenate(out, axis=1)

    def before_0(n, count):
        return older[:, lanes_at(n, count)]

    def before_1(n, count):
        return state[:, lanes_at(n + 1, count)]

    group = 4

    def run(now, before, out, shift, start, stop):
        whole = (stop - start) // group

        def one(g, carry):
            n = start + g * group
            out[:, lanes_at(n + shift, group)] = stepped(now, before, n, group)
            return carry

        lax.fori_loop(0, whole, one, 0)
        n, count = start + whole * group, stop - start - whole * group
        if count:
            out[:, lanes_at(n + shift, count)] = stepped(now, before, n, count)

    get_state.wait()
    get_older.wait()
    up[0].wait_recv()
    down[0].wait_recv()
    base[...] = stepped(state, before_0, 0, itiles, first=True)
    run(state, before_0, newer, 1, itiles, tiles - 1)
    newer[:, pl.ds(tiles * LANES, LANES)] = stepped(state, before_0, tiles - 1, 1, last=True)
    up[1].start()

    def put(src, dst, n):
        copy = pltpu.make_async_copy(src, dst, out_sem.at[n])
        copy.start()
        return copy

    puts = [put(tile(newer, 1 + itiles, tiles - itiles), tile(prior.at[0], itiles, tiles - itiles), 0)]
    all_of(labels, labels_in, ITERS).wait_recv()
    got = labels_in[...].reshape(iface, LANES)
    f = iota((iface, iface), 1)
    place[0:iface, :] = jnp.where(got[:, 0:1] == f, 1.0, 0.0).astype(BF16)
    half = LANES // 2
    place[iface:, :] = jnp.where(got[:, half : half + 1] == f, 1.0, 0.0).astype(BF16)
    run(newer, before_1, final, 0, itiles + 1, tiles - 1)
    puts.append(
        put(tile(final, itiles + 1, tiles - itiles - 2), tile(latest.at[0], itiles + 1, tiles - itiles - 2), 1)
    )

    def forced(step):
        all_of(packed.at[step], arrived.at[step], step).wait_recv()
        got = arrived[step].reshape(iface, LANES).T
        high, low = halves(got)
        both = jnp.concatenate(
            [jnp.concatenate([v[:half], v[half:]], axis=1) for v in (high, low)], axis=0
        )
        out = dot(both, place[...])
        return base[...] + DT2 * (out[:rows] + out[rows:])

    mid = forced(0)
    newer[:, pl.ds(LANES, iface)] = mid
    traces(mid, 1)
    for k in ways:
        part_copy(1, k).start()
    down[1].start()
    puts.append(put(tile(newer, 1, itiles), tile(prior.at[0], 0, itiles), 2))

    up[1].wait_recv()
    ahead = stepped(newer, before_1, 0, itiles + 1, first=True)
    base[...] = ahead[:, :iface]
    final[:, pl.ds(iface, LANES)] = ahead[:, iface:]
    puts.append(put(tile(final, itiles), tile(latest.at[0], itiles), 3))

    exchange(1)
    down[1].wait_recv()
    final[:, pl.ds((tiles - 1) * LANES, LANES)] = stepped(newer, before_1, tiles - 1, 1, last=True)
    puts.append(put(tile(final, tiles - 1), tile(latest.at[0], tiles - 1), 4))

    final[:, pl.ds(0, iface)] = forced(1)
    puts.append(put(tile(final, 0, itiles), tile(latest.at[0], 0, itiles), 5))
    for step in range(ITERS):
        for k in ways:
            part_copy(step, k).wait_send()
        all_of(packed.at[step], arrived.at[step], step).wait_send()
        up[step].wait_send()
        down[step].wait_send()
    all_of(labels, labels_in, ITERS).wait_send()
    for copy in puts:
        copy.wait()


ITERS = 2
DT2 = 0.5
KAPPA = 0.5


def body(mesh_shape, field, previous, stiff, synth, owner, face, weight):
    domains, nsub = mesh_shape["mer"], mesh_shape["sub"]
    nz = 1 << (int(math.log2(domains)) // 2)
    ny = domains // nz
    _, rows, points = field.shape
    iface = owner.shape[1]
    height = iface // domains
    edge = stiff.shape[1]
    dma = pltpu.SemaphoreType.DMA
    any_space = pl.BlockSpec(memory_space=pl.ANY)
    blocks = (domains, height, LANES)
    scratch = [
        pltpu.VMEM((rows, points + 2 * LANES), F32),
        pltpu.VMEM((rows, points), F32),
        pltpu.VMEM((rows, points + 2 * LANES), F32),
        pltpu.VMEM((rows, points), F32),
        pltpu.VMEM((edge, edge), F32),
        pltpu.VMEM((rows, nsub * rows), F32),
        pltpu.VMEM((1, iface), jnp.int32),
        pltpu.VMEM((1, iface), jnp.int32),
        pltpu.VMEM((1, iface), F32),
        pltpu.VMEM((ITERS, nsub, rows, iface), F32),
        pltpu.VMEM((ITERS, nsub - 1, rows, iface), F32),
        pltpu.VMEM((ITERS, *blocks), F32),
        pltpu.VMEM((ITERS, *blocks), F32),
        pltpu.VMEM(blocks, F32),
        pltpu.VMEM(blocks, F32),
        pltpu.VMEM((2 * edge, 2 * edge), BF16),
        pltpu.VMEM((nsub * rows, 4 * rows), BF16),
        pltpu.VMEM((2 * iface, iface), BF16),
        pltpu.VMEM((2 * iface, iface), BF16),
        pltpu.VMEM((rows, iface), F32),
        dma((8,)),
        dma((ITERS, nsub - 1)),
        dma((ITERS, nsub - 1)),
        dma((ITERS + 1,)),
        dma((ITERS + 1,)),
        dma((ITERS, 2)),
        dma((ITERS, 2)),
        pltpu.SemaphoreType.REGULAR,
        dma((6,)),
    ]
    out = jax.ShapeDtypeStruct(field.shape, F32)
    return pl.pallas_call(
        functools.partial(kernel, ny, nz, nsub),
        out_shape=(out, out),
        in_specs=[any_space] * 7,
        out_specs=(any_space, any_space),
        scratch_shapes=scratch,
        compiler_params=pltpu.CompilerParams(
            collective_id=0, has_side_effects=True, vmem_limit_bytes=40 << 20
        ),
    )(
        field, previous, stiff, jnp.swapaxes(synth, 1, 2), owner.reshape(1, iface), face, weight
    )


def solution(mesh):
    in_specs = (
        P("grp", "sub", "mer"),
        P("grp", "sub", "mer"),
        P("grp", None, None),
        P("grp", None, "sub"),
        P("grp", "mer", None),
        P("grp", "mer"),
        P("grp", "mer"),
    )
    out_specs = (P("grp", "sub", "mer"), P("grp", "sub", "mer"))
    return jax.shard_map(
        functools.partial(body, dict(mesh.shape)),
        mesh=mesh,
        in_specs=in_specs,
        out_specs=out_specs,
        check_vma=False,
    )
```

```python
import functools
import math

import jax
import jax.numpy as jnp
from jax import lax
from jax.experimental import pallas as pl
from jax.experimental.pallas import tpu as pltpu
from jax.sharding import PartitionSpec as P

MESH = pl.DeviceIdType.MESH
F32, BF16 = jnp.float32, jnp.bfloat16
LANES = 128
NT = (((1,), (1,)), ((), ()))


def halves(value):
    high = value.astype(BF16)
    return high, (value - high.astype(F32)).astype(BF16)


def iota(shape, dim):
    return lax.broadcasted_iota(jnp.int32, shape, dim).astype(F32)


def lanes_at(n, count):
    start = n * LANES
    return pl.ds(start if isinstance(n, int) else pl.multiple_of(start, LANES), count * LANES)


def dot(a, b):
    return jnp.dot(a, b, preferred_element_type=F32)


def kernel(
    ny, nz, nsub, field, previous, stiff, synth_t, owner, face, weight, final, newer,
    state, older, halo, stiff_v, synth_v, owner_v, face_v, weight_v,
    part, part_in, packed, arrived, labels, labels_in,
    element, operator, pick, place, base,
    load_sem, part_send, part_recv, pack_send, pack_recv, halo_send, halo_recv, near_sem,
):
    rows, points = older.shape
    tiles = points // LANES
    domains, height, _ = labels.shape
    iface = domains * height
    itiles = iface // LANES
    grp, mer, sub = lax.axis_index("grp"), lax.axis_index("mer"), lax.axis_index("sub")
    other = 1 - grp
    y, z = mer // nz, mer % nz
    above, below = (mer + 1) % domains, (mer + domains - 1) % domains

    barrier = pltpu.get_barrier_semaphore()

    def greet(sem, **where):
        pl.semaphore_signal(sem, inc=1, device_id=where, device_id_type=MESH)

    for k in range(1, nsub):
        greet(barrier, grp=grp, mer=mer, sub=(sub + k) % nsub)
    for k in range(1, nz):
        greet(barrier, grp=grp, mer=y * nz + (z + k) % nz, sub=sub)
    for k in range(ny):
        greet(barrier, grp=other, mer=(y + k) % ny * nz + z, sub=sub)
    greet(barrier, grp=grp, mer=above, sub=sub)
    greet(barrier, grp=grp, mer=below, sub=sub)

    def load(src, dst, n):
        copy = pltpu.make_async_copy(src, dst, load_sem.at[n])
        copy.start()
        return copy

    get_synth = load(synth_t.at[0], synth_v, 0)
    get_iface = load(field.at[0, :, pl.ds(0, iface)], state.at[:, pl.ds(0, iface)], 1)
    get_owner = load(owner, owner_v, 2)
    get_face = load(face, face_v, 3)
    get_weight = load(weight, weight_v, 4)
    get_stiff = load(stiff.at[0], stiff_v, 5)
    get_state = load(
        field.at[0, :, pl.ds(iface, points - iface)], state.at[:, pl.ds(iface, points - iface)], 6
    )
    get_older = load(previous.at[0], older, 7)

    def traces(value, step):
        high, low = halves(value)
        sums = dot(operator[...], jnp.concatenate([high, low, high, low], axis=0))
        part[step] = sums.reshape(nsub, rows, iface)

    def part_copy(step, k):
        to = (sub + k) % nsub
        return pltpu.make_async_remote_copy(
            src_ref=part.at[step, to],
            dst_ref=part_in.at[step, k - 1],
            send_sem=part_send.at[step, k - 1],
            recv_sem=part_recv.at[step, k - 1],
            device_id={"grp": grp, "mer": mer, "sub": to},
            device_id_type=MESH,
        )

    ways = sorted(range(1, nsub), key=lambda k: -min(k, nsub - k))

    get_synth.wait()
    high, low = halves(synth_v[...])
    high, low = high.astype(F32), low.astype(F32)
    operator[...] = jnp.concatenate([high, high, low, low], axis=0).T.astype(BF16)
    get_iface.wait()
    traces(state[:, :iface], 0)

    pl.semaphore_wait(barrier, nsub - 1 + nz - 1 + ny + 2)
    for k in ways:
        part_copy(0, k).start()
    for k in range(ny):
        greet(near_sem, grp=other, mer=(y + k) % ny * nz + z, sub=sub)

    def halo_copy(src, dst, to, step, way):
        return pltpu.make_async_remote_copy(
            src_ref=src,
            dst_ref=dst,
            send_sem=halo_send.at[step, way],
            recv_sem=halo_recv.at[step, way],
            device_id={"grp": grp, "mer": to, "sub": sub},
            device_id_type=MESH,
        )

    def lanes_of(ref, n):
        return ref.at[:, pl.ds(n * LANES, LANES)]

    up = [
        halo_copy(lanes_of(field.at[0], tiles - 1), halo.at[0, 0], above, 0, 0),
        halo_copy(lanes_of(newer, tiles - 1), halo.at[1, 0], above, 1, 0),
    ]
    down = [
        halo_copy(lanes_of(field.at[0], 0), halo.at[0, 1], below, 0, 1),
        halo_copy(lanes_of(newer, 0), halo.at[1, 1], below, 1, 1),
    ]
    up[0].start()
    down[0].start()

    get_owner.wait()
    get_face.wait()
    get_weight.wait()
    own = owner_v[...].astype(F32)
    across = jnp.broadcast_to(own, (iface, iface))
    i, j = iota((iface, iface), 0), iota((iface, iface), 1)
    down_own = jnp.sum(jnp.where(i == j, across, 0.0), axis=1, keepdims=True)
    rank = jnp.sum(jnp.where((down_own == across) & (i < j), 1.0, 0.0), axis=0, keepdims=True)
    second = (rank >= height).astype(F32)
    row = own * height + rank - height * second
    hit = jnp.where(i == row, 1.0, 0.0)
    pick[0:iface, :] = (hit * (1.0 - second)).astype(BF16)
    pick[iface:, :] = (hit * second).astype(BF16)
    left_half = lax.broadcasted_iota(jnp.int32, (iface, LANES), 1) < LANES // 2
    names = jnp.broadcast_to(face_v[...].astype(F32), (LANES, iface)).astype(BF16)
    named = lax.dot_general(pick[...], names, NT, preferred_element_type=F32)
    labels[...] = jnp.where(left_half, named[:iface], named[iface:]).reshape(labels.shape)

    def owner_copy(src, dst, n, k):
        to = (y + ny // 2 + k // nz) % ny * nz + (z + nz // 2 + k % nz) % nz
        return pltpu.make_async_remote_copy(
            src_ref=src.at[to],
            dst_ref=dst.at[mer],
            send_sem=pack_send.at[n],
            recv_sem=pack_recv.at[n],
            device_id={"grp": other, "mer": to, "sub": sub},
            device_id_type=MESH,
        )

    def send_all(src, dst, n):
        def one(k, carry):
            owner_copy(src, dst, n, k).start()
            return carry

        lax.fori_loop(0, domains, one, 0, unroll=8)

    def all_of(src, dst, n):
        return pltpu.make_async_remote_copy(
            src_ref=src,
            dst_ref=dst,
            send_sem=pack_send.at[n],
            recv_sem=pack_recv.at[n],
            device_id={"grp": other, "mer": mer, "sub": sub},
            device_id_type=MESH,
        )

    pl.semaphore_wait(near_sem, ny)
    send_all(labels, labels_in, ITERS)

    def exchange(step):
        total = part[step, sub]
        for k in ways[::-1]:
            part_copy(step, k).wait_recv()
            total = total + part_in[step, k - 1]
        total = total * weight_v[...]
        high, low = halves(total)
        both = jnp.concatenate([high, low], axis=0)
        out = lax.dot_general(pick[...], both, NT, preferred_element_type=F32)
        out = out + pltpu.roll(out, LANES // 2, 1)
        packed[step] = jnp.where(left_half, out[:iface], out[iface:]).reshape(labels.shape)
        send_all(packed.at[step], arrived.at[step], step)

    exchange(0)

    get_stiff.wait()
    high, low = halves(stiff_v[...] * DT2)
    both = jnp.concatenate([high, low], axis=1)
    element[...] = jnp.concatenate([both, both], axis=0)
    lane = lax.broadcasted_iota(jnp.int32, (rows, LANES), 1)
    inner_low = jnp.where(mer > 0, 1.0, 0.0)
    inner_high = jnp.where(mer < domains - 1, 1.0, 0.0)

    def stepped(step, n, count):
        now, before = ((state, older), (newer, state))[step]
        static = isinstance(n, int)
        first, last = static and n == 0, static and n + count == tiles
        chunk = now[:, lanes_at(n if first else n - 1, count + 2 - first - last)]
        x = [chunk[:, LANES * c : LANES * (c + 1)] for c in range(chunk.shape[1] // LANES)]
        if first:
            x = [halo[step, 0] * inner_low] + x
        if last:
            x = x + [halo[step, 1] * inner_high]
        old = before[:, lanes_at(n, count)]
        high, low = halves(jnp.concatenate(x[1:-1], axis=0))
        product = dot(jnp.concatenate([high, low], axis=1), element[...])
        product = product[:, :LANES] + product[:, LANES:]
        right = [pltpu.roll(v, 1, 1) for v in x[:-1]]
        left = [pltpu.roll(v, LANES - 1, 1) for v in x[1:]]
        out = []
        for c in range(count):
            lower = jnp.where(lane == 0, right[c], right[c + 1])
            upper = jnp.where(lane == LANES - 1, left[c + 1], left[c])
            v = x[c + 1]
            lap = 2.0 * v - lower - upper
            out.append(
                2.0 * v - old[:, LANES * c : LANES * (c + 1)]
                - product[rows * c : rows * (c + 1)] - (DT2 * KAPPA) * lap
            )
        return jnp.concatenate(out, axis=1)

    group = 4

    def run(step, out, start, stop):
        whole = (stop - start) // group

        def one(g, carry):
            n = start + g * group
            out[:, lanes_at(n, group)] = stepped(step, n, group)
            return carry

        lax.fori_loop(0, whole, one, 0)
        n, count = start + whole * group, stop - start - whole * group
        if count:
            out[:, lanes_at(n, count)] = stepped(step, n, count)

    get_state.wait()
    get_older.wait()
    up[0].wait_recv()
    down[0].wait_recv()
    base[...] = stepped(0, 0, itiles)
    run(0, newer, itiles, tiles - 1)
    newer[:, pl.ds((tiles - 1) * LANES, LANES)] = stepped(0, tiles - 1, 1)
    up[1].start()

    all_of(labels, labels_in, ITERS).wait_recv()
    got = labels_in[...].reshape(iface, LANES)
    f = iota((iface, iface), 1)
    place[0:iface, :] = jnp.where(got[:, 0:1] == f, 1.0, 0.0).astype(BF16)
    half = LANES // 2
    place[iface:, :] = jnp.where(got[:, half : half + 1] == f, 1.0, 0.0).astype(BF16)
    run(1, final, itiles + 1, tiles - 1)

    def forced(step):
        all_of(packed.at[step], arrived.at[step], step).wait_recv()
        got = arrived[step].reshape(iface, LANES).T
        high, low = halves(got)
        both = jnp.concatenate(
            [jnp.concatenate([v[:half], v[half:]], axis=1) for v in (high, low)], axis=0
        )
        out = dot(both, place[...])
        return base[...] + DT2 * (out[:rows] + out[rows:])

    mid = forced(0)
    newer[:, pl.ds(0, iface)] = mid
    traces(mid, 1)
    for k in ways:
        part_copy(1, k).start()
    down[1].start()

    up[1].wait_recv()
    ahead = stepped(1, 0, itiles + 1)
    base[...] = ahead[:, :iface]
    final[:, pl.ds(iface, LANES)] = ahead[:, iface:]

    exchange(1)
    down[1].wait_recv()
    final[:, pl.ds((tiles - 1) * LANES, LANES)] = stepped(1, tiles - 1, 1)

    final[:, pl.ds(0, iface)] = forced(1)
    for step in range(ITERS):
        for k in ways:
            part_copy(step, k).wait_send()
        all_of(packed.at[step], arrived.at[step], step).wait_send()
        up[step].wait_send()
        down[step].wait_send()
    all_of(labels, labels_in, ITERS).wait_send()

def written(final, newer, latest, prior, sem):
    copies = [
        pltpu.make_async_copy(src, dst.at[0], sem.at[n])
        for n, (src, dst) in enumerate(((final, latest), (newer, prior)))
    ]
    for copy in copies:
        copy.start()
    for copy in copies:
        copy.wait()


ITERS = 2
DT2 = 0.5
KAPPA = 0.5
RESERVED = 64900000


def body(mesh_shape, field, previous, stiff, synth, owner, face, weight):
    domains, nsub = mesh_shape["mer"], mesh_shape["sub"]
    nz = 1 << (int(math.log2(domains)) // 2)
    ny = domains // nz
    _, rows, points = field.shape
    iface = owner.shape[1]
    height = iface // domains
    edge = stiff.shape[1]
    dma = pltpu.SemaphoreType.DMA
    anywhere = pl.BlockSpec(memory_space=pl.ANY)
    vmem = pl.BlockSpec(memory_space=pltpu.VMEM)
    blocks = (domains, height, LANES)
    scratch = [
        pltpu.VMEM((rows, points), F32),
        pltpu.VMEM((rows, points), F32),
        pltpu.VMEM((ITERS, 2, rows, LANES), F32),
        pltpu.VMEM((edge, edge), F32),
        pltpu.VMEM((rows, nsub * rows), F32),
        pltpu.VMEM((1, iface), jnp.int32),
        pltpu.VMEM((1, iface), jnp.int32),
        pltpu.VMEM((1, iface), F32),
        pltpu.VMEM((ITERS, nsub, rows, iface), F32),
        pltpu.VMEM((ITERS, nsub - 1, rows, iface), F32),
        pltpu.VMEM((ITERS, *blocks), F32),
        pltpu.VMEM((ITERS, *blocks), F32),
        pltpu.VMEM(blocks, F32),
        pltpu.VMEM(blocks, F32),
        pltpu.VMEM((2 * edge, 2 * edge), BF16),
        pltpu.VMEM((nsub * rows, 4 * rows), BF16),
        pltpu.VMEM((2 * iface, iface), BF16),
        pltpu.VMEM((2 * iface, iface), BF16),
        pltpu.VMEM((rows, iface), F32),
        dma((8,)),
        dma((ITERS, nsub - 1)),
        dma((ITERS, nsub - 1)),
        dma((ITERS + 1,)),
        dma((ITERS + 1,)),
        dma((ITERS, 2)),
        dma((ITERS, 2)),
        pltpu.SemaphoreType.REGULAR,
    ]
    stepped = pl.pallas_call(
        functools.partial(kernel, ny, nz, nsub),
        out_shape=(pltpu.VMEM((rows, points), F32),) * 2,
        in_specs=[anywhere] * 7,
        out_specs=(vmem, vmem),
        scratch_shapes=scratch,
        compiler_params=pltpu.CompilerParams(
            collective_id=0, has_side_effects=True, vmem_limit_bytes=RESERVED
        ),
    )(
        field, previous, stiff, jnp.swapaxes(synth, 1, 2), owner.reshape(1, iface), face, weight
    )
    out = jax.ShapeDtypeStruct(field.shape, F32)
    return pl.pallas_call(
        written,
        out_shape=(out, out),
        in_specs=[anywhere] * 2,
        out_specs=(anywhere, anywhere),
        scratch_shapes=[dma((2,))],
        compiler_params=pltpu.CompilerParams(vmem_limit_bytes=1 << 20),
    )(*stepped)


def solution(mesh):
    in_specs = (
        P("grp", "sub", "mer"),
        P("grp", "sub", "mer"),
        P("grp", None, None),
        P("grp", None, "sub"),
        P("grp", "mer", None),
        P("grp", "mer"),
        P("grp", "mer"),
    )
    out_specs = (P("grp", "sub", "mer"), P("grp", "sub", "mer"))
    return jax.shard_map(
        functools.partial(body, dict(mesh.shape)),
        mesh=mesh,
        in_specs=in_specs,
        out_specs=out_specs,
        check_vma=False,
    )
```

```python
import functools
import math

import jax
import jax.numpy as jnp
from jax import lax
from jax.experimental import pallas as pl
from jax.experimental.pallas import tpu as pltpu
from jax.sharding import PartitionSpec as P

MESH = pl.DeviceIdType.MESH
F32, BF16 = jnp.float32, jnp.bfloat16
LANES = 128
NT = (((1,), (1,)), ((), ()))


def halves(value):
    high = value.astype(BF16)
    return high, (value - high.astype(F32)).astype(BF16)


def iota(shape, dim):
    return lax.broadcasted_iota(jnp.int32, shape, dim).astype(F32)


def lanes_at(n, count):
    start = n * LANES
    return pl.ds(start if isinstance(n, int) else pl.multiple_of(start, LANES), count * LANES)


def dot(a, b):
    return jnp.dot(a, b, preferred_element_type=F32)


def kernel(
    ny, nz, nsub, field, previous, stiff, synth_t, owner, face, weight, final, newer,
    state, older, halo, stiff_v, synth_v, owner_v, face_v, weight_v,
    part, part_in, first, first_in, second, second_in,
    element, operator, pick, place, base,
    load_sem, part_send, part_recv, pack_send, pack_recv, halo_send, halo_recv, near_sem,
):
    rows, points = older.shape
    tiles = points // LANES
    domains, height, _ = second.shape
    iface = domains * height
    itiles = iface // LANES
    grp, mer, sub = lax.axis_index("grp"), lax.axis_index("mer"), lax.axis_index("sub")
    other = 1 - grp
    y, z = mer // nz, mer % nz
    above, below = (mer + 1) % domains, (mer + domains - 1) % domains

    barrier = pltpu.get_barrier_semaphore()

    def greet(sem, **where):
        pl.semaphore_signal(sem, inc=1, device_id=where, device_id_type=MESH)

    def load(src, dst, n):
        copy = pltpu.make_async_copy(src, dst, load_sem.at[n])
        copy.start()
        return copy

    get_synth = load(synth_t.at[0], synth_v, 0)
    get_iface = load(field.at[0, :, pl.ds(0, iface)], state.at[:, pl.ds(0, iface)], 1)
    get_owner = load(owner, owner_v, 2)
    get_face = load(face, face_v, 3)
    get_weight = load(weight, weight_v, 4)
    get_stiff = load(stiff.at[0], stiff_v, 5)
    get_state = load(
        field.at[0, :, pl.ds(iface, points - iface)], state.at[:, pl.ds(iface, points - iface)], 6
    )
    get_older = load(previous.at[0], older, 7)

    for k in range(1, nsub):
        greet(barrier, grp=grp, mer=mer, sub=(sub + k) % nsub)
    for k in range(1, nz):
        greet(barrier, grp=grp, mer=y * nz + (z + k) % nz, sub=sub)
    for k in range(ny):
        greet(barrier, grp=other, mer=(y + k) % ny * nz + z, sub=sub)
    greet(barrier, grp=grp, mer=above, sub=sub)
    greet(barrier, grp=grp, mer=below, sub=sub)

    def traces(value, step):
        high, low = halves(value)
        sums = dot(operator[...], jnp.concatenate([high, low, high, low], axis=0))
        part[step] = sums.reshape(nsub, rows, iface)

    def part_copy(step, k):
        to = (sub + k) % nsub
        return pltpu.make_async_remote_copy(
            src_ref=part.at[step, to],
            dst_ref=part_in.at[step, k - 1],
            send_sem=part_send.at[step, k - 1],
            recv_sem=part_recv.at[step, k - 1],
            device_id={"grp": grp, "mer": mer, "sub": to},
            device_id_type=MESH,
        )

    ways = sorted(range(1, nsub), key=lambda k: -min(k, nsub - k))

    get_synth.wait()
    high, low = halves(synth_v[...])
    high, low = high.astype(F32), low.astype(F32)
    operator[...] = jnp.concatenate([high, high, low, low], axis=0).T.astype(BF16)
    get_iface.wait()
    traces(state[:, :iface], 0)

    pl.semaphore_wait(barrier, nsub - 1 + nz - 1 + ny + 2)
    for k in ways:
        part_copy(0, k).start()
    for k in range(ny):
        greet(near_sem, grp=other, mer=(y + k) % ny * nz + z, sub=sub)

    def halo_copy(src, dst, to, step, way):
        return pltpu.make_async_remote_copy(
            src_ref=src,
            dst_ref=dst,
            send_sem=halo_send.at[step, way],
            recv_sem=halo_recv.at[step, way],
            device_id={"grp": grp, "mer": to, "sub": sub},
            device_id_type=MESH,
        )

    def lanes_of(ref, n):
        return ref.at[:, pl.ds(n * LANES, LANES)]

    up = [
        halo_copy(lanes_of(field.at[0], tiles - 1), halo.at[0, 0], above, 0, 0),
        halo_copy(lanes_of(newer, tiles - 1), halo.at[1, 0], above, 1, 0),
    ]
    down = [
        halo_copy(lanes_of(field.at[0], 0), halo.at[0, 1], below, 0, 1),
        halo_copy(lanes_of(newer, 0), halo.at[1, 1], below, 1, 1),
    ]
    up[0].start()
    down[0].start()

    get_owner.wait()
    get_face.wait()
    get_weight.wait()
    own = owner_v[...].astype(F32)
    across = jnp.broadcast_to(own, (iface, iface))
    i, j = iota((iface, iface), 0), iota((iface, iface), 1)
    down_own = jnp.sum(jnp.where(i == j, across, 0.0), axis=1, keepdims=True)
    rank = jnp.sum(jnp.where((down_own == across) & (i < j), 1.0, 0.0), axis=0, keepdims=True)
    late = (rank >= height).astype(F32)
    row = own * height + rank - height * late
    hit = jnp.where(i == row, 1.0, 0.0)
    pick[0:iface, :] = (hit * (1.0 - late)).astype(BF16)
    pick[iface:, :] = (hit * late).astype(BF16)
    left_half = lax.broadcasted_iota(jnp.int32, (iface, LANES), 1) < LANES // 2

    named = jnp.where(iota((LANES, iface), 0) == rank, face_v[...].astype(F32), 0.0).astype(BF16)
    chosen = jnp.where(iota((domains, iface), 0) == own, 1.0, 0.0).astype(BF16)
    names = lax.dot_general(chosen, named, NT, preferred_element_type=F32)
    first[:, pl.ds(height, 1), :] = names.reshape(domains, 1, LANES)

    offsets = [(a, b) for a in range(ny) for b in range(nz)]
    offsets.sort(key=lambda o: -(min(o[0], ny - o[0]) + min(o[1], nz - o[1])))
    y_at = [(y + a) % ny * nz for a in range(ny)]
    z_at = [(z + b) % nz for b in range(nz)]
    sent, landed = (first, second), (first_in, second_in)

    def send_all(step):
        for a, b in offsets:
            to = y_at[a] + z_at[b]
            pltpu.make_async_remote_copy(
                src_ref=sent[step].at[to],
                dst_ref=landed[step].at[mer],
                send_sem=pack_send.at[step],
                recv_sem=pack_recv.at[step],
                device_id={"grp": other, "mer": to, "sub": sub},
                device_id_type=MESH,
            ).start()

    def all_of(step):
        return pltpu.make_async_remote_copy(
            src_ref=sent[step],
            dst_ref=landed[step],
            send_sem=pack_send.at[step],
            recv_sem=pack_recv.at[step],
            device_id={"grp": other, "mer": mer, "sub": sub},
            device_id_type=MESH,
        )

    def exchange(step):
        total = part[step, sub]
        for k in ways[::-1]:
            part_copy(step, k).wait_recv()
            total = total + part_in[step, k - 1]
        total = total * weight_v[...]
        high, low = halves(total)
        both = jnp.concatenate([high, low], axis=0)
        out = lax.dot_general(pick[...], both, NT, preferred_element_type=F32)
        out = out + pltpu.roll(out, LANES // 2, 1)
        out = jnp.where(left_half, out[:iface], out[iface:])
        sent[step][:, pl.ds(0, height), :] = out.reshape(domains, height, LANES)
        if step == 0:
            pl.semaphore_wait(near_sem, ny)
        send_all(step)

    exchange(0)

    get_stiff.wait()
    high, low = halves(stiff_v[...] * DT2)
    both = jnp.concatenate([high, low], axis=1)
    element[...] = jnp.concatenate([both, both], axis=0)
    lane = lax.broadcasted_iota(jnp.int32, (rows, LANES), 1)
    inner_low = jnp.where(mer > 0, 1.0, 0.0)
    inner_high = jnp.where(mer < domains - 1, 1.0, 0.0)

    def stepped(step, n, count):
        now, before = ((state, older), (newer, state))[step]
        static = isinstance(n, int)
        first, last = static and n == 0, static and n + count == tiles
        chunk = now[:, lanes_at(n if first else n - 1, count + 2 - first - last)]
        x = [chunk[:, LANES * c : LANES * (c + 1)] for c in range(chunk.shape[1] // LANES)]
        if first:
            x = [halo[step, 0] * inner_low] + x
        if last:
            x = x + [halo[step, 1] * inner_high]
        old = before[:, lanes_at(n, count)]
        high, low = halves(jnp.concatenate(x[1:-1], axis=0))
        product = dot(jnp.concatenate([high, low], axis=1), element[...])
        product = product[:, :LANES] + product[:, LANES:]
        right = [pltpu.roll(v, 1, 1) for v in x[:-1]]
        left = [pltpu.roll(v, LANES - 1, 1) for v in x[1:]]
        out = []
        for c in range(count):
            lower = jnp.where(lane == 0, right[c], right[c + 1])
            upper = jnp.where(lane == LANES - 1, left[c + 1], left[c])
            v = x[c + 1]
            lap = 2.0 * v - lower - upper
            out.append(
                2.0 * v - old[:, LANES * c : LANES * (c + 1)]
                - product[rows * c : rows * (c + 1)] - (DT2 * KAPPA) * lap
            )
        return jnp.concatenate(out, axis=1)

    group = 4

    def run(step, out, start, stop):
        whole = (stop - start) // group

        def one(g, carry):
            n = start + g * group
            out[:, lanes_at(n, group)] = stepped(step, n, group)
            return carry

        lax.fori_loop(0, whole, one, 0)
        n, count = start + whole * group, stop - start - whole * group
        if count:
            out[:, lanes_at(n, count)] = stepped(step, n, count)

    get_state.wait()
    get_older.wait()
    up[0].wait_recv()
    down[0].wait_recv()
    base[...] = stepped(0, 0, itiles)
    run(0, newer, itiles, tiles - 1)
    newer[:, pl.ds((tiles - 1) * LANES, LANES)] = stepped(0, tiles - 1, 1)
    up[1].start()

    run(1, final, itiles + 1, tiles - 1)

    half = LANES // 2
    block = lax.broadcasted_iota(jnp.int32, (iface, domains), 0) // height
    spread = jnp.where(block == lax.broadcasted_iota(jnp.int32, (iface, domains), 1), 1.0, 0.0).astype(BF16)
    slot = lax.broadcasted_iota(jnp.int32, (iface, LANES), 1)
    slot = slot - lax.broadcasted_iota(jnp.int32, (iface, LANES), 0) % height

    def placed():
        names = first_in[:, pl.ds(height, 1), :].reshape(domains, LANES)
        names = dot(spread, names.astype(BF16))
        f = iota((iface, iface), 1)
        for n in range(2):
            name = jnp.sum(jnp.where(slot == n * height, names, 0.0), axis=1, keepdims=True)
            place[n * iface : (n + 1) * iface, :] = jnp.where(name == f, 1.0, 0.0).astype(BF16)

    def forced(step):
        all_of(step).wait_recv()
        if step == 0:
            placed()
        got = landed[step][:, pl.ds(0, height), :].reshape(iface, LANES).T
        high, low = halves(got)
        both = jnp.concatenate(
            [jnp.concatenate([v[:half], v[half:]], axis=1) for v in (high, low)], axis=0
        )
        out = dot(both, place[...])
        return base[...] + DT2 * (out[:rows] + out[rows:])

    mid = forced(0)
    newer[:, pl.ds(0, iface)] = mid
    traces(mid, 1)
    for k in ways:
        part_copy(1, k).start()
    down[1].start()

    up[1].wait_recv()
    ahead = stepped(1, 0, itiles + 1)
    base[...] = ahead[:, :iface]
    final[:, pl.ds(iface, LANES)] = ahead[:, iface:]

    exchange(1)
    down[1].wait_recv()
    final[:, pl.ds((tiles - 1) * LANES, LANES)] = stepped(1, tiles - 1, 1)

    final[:, pl.ds(0, iface)] = forced(1)
    for step in range(ITERS):
        for k in ways:
            part_copy(step, k).wait_send()
        all_of(step).wait_send()
        up[step].wait_send()
        down[step].wait_send()

def written(final, newer, latest, prior, sem):
    step = final.shape[0] // CHUNKS
    copies = [
        pltpu.make_async_copy(
            src.at[pl.ds(c * step, step)], dst.at[0, pl.ds(c * step, step)], sem.at[n, c]
        )
        for c in range(CHUNKS)
        for n, (src, dst) in enumerate(((final, latest), (newer, prior)))
    ]
    for copy in copies:
        copy.start()
    for copy in copies:
        copy.wait()


CHUNKS = 1
ITERS = 2
DT2 = 0.5
KAPPA = 0.5
RESERVED = 64900000


def body(mesh_shape, field, previous, stiff, synth, owner, face, weight):
    domains, nsub = mesh_shape["mer"], mesh_shape["sub"]
    nz = 1 << (int(math.log2(domains)) // 2)
    ny = domains // nz
    _, rows, points = field.shape
    iface = owner.shape[1]
    height = iface // domains
    edge = stiff.shape[1]
    dma = pltpu.SemaphoreType.DMA
    anywhere = pl.BlockSpec(memory_space=pl.ANY)
    vmem = pl.BlockSpec(memory_space=pltpu.VMEM)
    scratch = [
        pltpu.VMEM((rows, points), F32),
        pltpu.VMEM((rows, points), F32),
        pltpu.VMEM((ITERS, 2, rows, LANES), F32),
        pltpu.VMEM((edge, edge), F32),
        pltpu.VMEM((rows, nsub * rows), F32),
        pltpu.VMEM((1, iface), jnp.int32),
        pltpu.VMEM((1, iface), jnp.int32),
        pltpu.VMEM((1, iface), F32),
        pltpu.VMEM((ITERS, nsub, rows, iface), F32),
        pltpu.VMEM((ITERS, nsub - 1, rows, iface), F32),
        pltpu.VMEM((domains, height + 1, LANES), F32),
        pltpu.VMEM((domains, height + 1, LANES), F32),
        pltpu.VMEM((domains, height, LANES), F32),
        pltpu.VMEM((domains, height, LANES), F32),
        pltpu.VMEM((2 * edge, 2 * edge), BF16),
        pltpu.VMEM((nsub * rows, 4 * rows), BF16),
        pltpu.VMEM((2 * iface, iface), BF16),
        pltpu.VMEM((2 * iface, iface), BF16),
        pltpu.VMEM((rows, iface), F32),
        dma((8,)),
        dma((ITERS, nsub - 1)),
        dma((ITERS, nsub - 1)),
        dma((ITERS,)),
        dma((ITERS,)),
        dma((ITERS, 2)),
        dma((ITERS, 2)),
        pltpu.SemaphoreType.REGULAR,
    ]
    stepped = pl.pallas_call(
        functools.partial(kernel, ny, nz, nsub),
        out_shape=(pltpu.VMEM((rows, points), F32),) * 2,
        in_specs=[anywhere] * 7,
        out_specs=(vmem, vmem),
        scratch_shapes=scratch,
        compiler_params=pltpu.CompilerParams(
            collective_id=0, has_side_effects=True, vmem_limit_bytes=RESERVED
        ),
    )(
        field, previous, stiff, jnp.swapaxes(synth, 1, 2), owner.reshape(1, iface), face, weight
    )
    out = jax.ShapeDtypeStruct(field.shape, F32)
    return pl.pallas_call(
        written,
        out_shape=(out, out),
        in_specs=[anywhere] * 2,
        out_specs=(anywhere, anywhere),
        scratch_shapes=[dma((2, CHUNKS))],
        compiler_params=pltpu.CompilerParams(vmem_limit_bytes=1 << 20),
    )(*stepped)


def solution(mesh):
    in_specs = (
        P("grp", "sub", "mer"),
        P("grp", "sub", "mer"),
        P("grp", None, None),
        P("grp", None, "sub"),
        P("grp", "mer", None),
        P("grp", "mer"),
        P("grp", "mer"),
    )
    out_specs = (P("grp", "sub", "mer"), P("grp", "sub", "mer"))
    return jax.shard_map(
        functools.partial(body, dict(mesh.shape)),
        mesh=mesh,
        in_specs=in_specs,
        out_specs=out_specs,
        check_vma=False,
    )
```

```python
import functools
import math

import jax
import jax.numpy as jnp
from jax import lax
from jax.experimental import pallas as pl
from jax.experimental.pallas import tpu as pltpu
from jax.sharding import PartitionSpec as P

MESH = pl.DeviceIdType.MESH
F32, BF16 = jnp.float32, jnp.bfloat16
LANES = 128
NT = (((1,), (1,)), ((), ()))


def halves(value):
    high = value.astype(BF16)
    return high, (value - high.astype(F32)).astype(BF16)


def iota(shape, dim):
    return lax.broadcasted_iota(jnp.int32, shape, dim).astype(F32)


def lanes_at(n, count):
    start = n * LANES
    return pl.ds(start if isinstance(n, int) else pl.multiple_of(start, LANES), count * LANES)


def dot(a, b):
    return jnp.dot(a, b, preferred_element_type=F32)


def kernel(
    ny, nz, nsub, field, previous, stiff, synth_t, owner, face, weight, final, newer,
    state, older, halo, stiff_v, synth_v, peer_v, owner_v, face_v, weight_v,
    part, part_in, first, first_in, second, second_in,
    element, operator, pick, place, base, ground,
    load_sem, part_send, part_recv, pack_send, pack_recv, halo_send, halo_recv, synth_send, synth_recv,
):
    rows, points = older.shape
    tiles = points // LANES
    domains, height, _ = second.shape
    iface = domains * height
    itiles = iface // LANES
    grp, mer, sub = lax.axis_index("grp"), lax.axis_index("mer"), lax.axis_index("sub")
    other = 1 - grp
    y, z = mer // nz, mer % nz
    above, below = (mer + 1) % domains, (mer + domains - 1) % domains

    barrier = pltpu.get_barrier_semaphore()

    def greet(sem, **where):
        pl.semaphore_signal(sem, inc=1, device_id=where, device_id_type=MESH)

    def load(src, dst, n):
        copy = pltpu.make_async_copy(src, dst, load_sem.at[n])
        copy.start()
        return copy

    get_synth = load(synth_t.at[0], synth_v.at[sub], 0)
    get_iface = load(field.at[0, :, pl.ds(0, iface)], state.at[:, pl.ds(0, iface)], 1)
    get_owner = load(owner, owner_v, 2)
    get_face = load(face, face_v, 3)
    get_weight = load(weight, weight_v, 4)
    get_stiff = load(stiff.at[0], stiff_v, 5)
    get_state = load(
        field.at[0, :, pl.ds(iface, points - iface)], state.at[:, pl.ds(iface, points - iface)], 6
    )
    get_older = load(previous.at[0], older, 7)

    offsets = [(a, b) for a in range(ny) for b in range(nz)]
    offsets.sort(key=lambda o: -(min(o[0], ny - o[0]) + min(o[1], nz - o[1])))
    y_at = [(y + a) % ny * nz for a in range(ny)]
    z_at = [(z + b) % nz for b in range(nz)]
    for a, b in offsets:
        greet(barrier, grp=other, mer=y_at[a] + z_at[b], sub=sub)
    for k in range(1, nsub):
        greet(barrier, grp=grp, mer=mer, sub=(sub + k) % nsub)
    greet(barrier, grp=grp, mer=above, sub=sub)
    greet(barrier, grp=grp, mer=below, sub=sub)

    def spread_out(value):
        high, low = halves(value)
        high, low = high.astype(F32), low.astype(F32)
        return jnp.concatenate([high, high, low, low], axis=0).T.astype(BF16)

    def doubled(value):
        high, low = halves(value)
        return jnp.concatenate([high, low, high, low], axis=0)

    def part_copy(step, k):
        to = (sub + k) % nsub
        return pltpu.make_async_remote_copy(
            src_ref=part.at[step, to],
            dst_ref=part_in.at[step, k - 1],
            send_sem=part_send.at[step, k - 1],
            recv_sem=part_recv.at[step, k - 1],
            device_id={"grp": grp, "mer": mer, "sub": to},
            device_id_type=MESH,
        )

    ways = sorted(range(1, nsub), key=lambda k: -min(k, nsub - k))

    def halo_copy(src, dst, to, step, way):
        return pltpu.make_async_remote_copy(
            src_ref=src,
            dst_ref=dst,
            send_sem=halo_send.at[step, way],
            recv_sem=halo_recv.at[step, way],
            device_id={"grp": grp, "mer": to, "sub": sub},
            device_id_type=MESH,
        )

    def lanes_of(ref, n):
        return ref.at[:, pl.ds(n * LANES, LANES)]

    up = [
        halo_copy(lanes_of(field.at[0], tiles - 1), halo.at[0, 0], above, 0, 0),
        halo_copy(lanes_of(newer, tiles - 1), halo.at[1, 0], above, 1, 0),
    ]
    down = [
        halo_copy(lanes_of(field.at[0], 0), halo.at[0, 1], below, 0, 1),
        halo_copy(lanes_of(newer, 0), halo.at[1, 1], below, 1, 1),
    ]
    get_owner.wait()
    get_face.wait()
    get_weight.wait()
    own = owner_v[...].astype(F32)
    across = jnp.broadcast_to(own, (iface, iface))
    i, j = iota((iface, iface), 0), iota((iface, iface), 1)
    down_own = jnp.sum(jnp.where(i == j, across, 0.0), axis=1, keepdims=True)
    rank = jnp.sum(jnp.where((down_own == across) & (i < j), 1.0, 0.0), axis=0, keepdims=True)
    late = (rank >= height).astype(F32)
    row = own * height + rank - height * late
    hit = jnp.where(i == row, 1.0, 0.0)
    pick[0:iface, :] = (hit * (1.0 - late)).astype(BF16)
    pick[iface:, :] = (hit * late).astype(BF16)
    left_half = lax.broadcasted_iota(jnp.int32, (iface, LANES), 1) < LANES // 2

    named = jnp.where(iota((LANES, iface), 0) == rank, face_v[...].astype(F32), 0.0).astype(BF16)
    chosen = jnp.where(iota((domains, iface), 0) == own, 1.0, 0.0).astype(BF16)
    names = lax.dot_general(chosen, named, NT, preferred_element_type=F32)
    first[:, pl.ds(height, 1), :] = names.reshape(domains, 1, LANES)

    sent, landed = (first, second), (first_in, second_in)

    def send_all(step):
        for a, b in offsets:
            to = y_at[a] + z_at[b]
            pltpu.make_async_remote_copy(
                src_ref=sent[step].at[to],
                dst_ref=landed[step].at[mer],
                send_sem=pack_send.at[step],
                recv_sem=pack_recv.at[step],
                device_id={"grp": other, "mer": to, "sub": sub},
                device_id_type=MESH,
            ).start()

    def all_of(step):
        return pltpu.make_async_remote_copy(
            src_ref=sent[step],
            dst_ref=landed[step],
            send_sem=pack_send.at[step],
            recv_sem=pack_recv.at[step],
            device_id={"grp": other, "mer": mer, "sub": sub},
            device_id_type=MESH,
        )

    def exchange(step, total):
        high, low = halves(total * weight_v[...])
        both = jnp.concatenate([high, low], axis=0)
        out = lax.dot_general(pick[...], both, NT, preferred_element_type=F32)
        out = out + pltpu.roll(out, LANES // 2, 1)
        out = jnp.where(left_half, out[:iface], out[iface:])
        sent[step][:, pl.ds(0, height), :] = out.reshape(domains, height, LANES)
        if step == 0:
            pl.semaphore_wait(barrier, domains + nsub - 1 + 2)
        send_all(step)

    def summed(n):
        total = part[n, sub]
        for k in ways[::-1]:
            part_copy(n, k).wait_recv()
            total = total + part_in[n, k - 1]
        return total

    get_stiff.wait()
    high, low = halves(stiff_v[...] * DT2)
    both = jnp.concatenate([high, low], axis=1)
    element[...] = jnp.concatenate([both, both], axis=0)
    lane = lax.broadcasted_iota(jnp.int32, (rows, LANES), 1)
    inner_low = jnp.where(mer > 0, 1.0, 0.0)
    inner_high = jnp.where(mer < domains - 1, 1.0, 0.0)

    def stepped(step, n, count):
        now, before = ((state, older), (newer, state))[step]
        static = isinstance(n, int)
        first, last = static and n == 0, static and n + count == tiles
        chunk = now[:, lanes_at(n if first else n - 1, count + 2 - first - last)]
        x = [chunk[:, LANES * c : LANES * (c + 1)] for c in range(chunk.shape[1] // LANES)]
        if first:
            x = [halo[step, 0] * inner_low] + x
        if last:
            x = x + [halo[step, 1] * inner_high]
        old = before[:, lanes_at(n, count)]
        high, low = halves(jnp.concatenate(x[1:-1], axis=0))
        product = dot(jnp.concatenate([high, low], axis=1), element[...])
        product = product[:, :LANES] + product[:, LANES:]
        right = [pltpu.roll(v, 1, 1) for v in x[:-1]]
        left = [pltpu.roll(v, LANES - 1, 1) for v in x[1:]]
        out = []
        for c in range(count):
            lower = jnp.where(lane == 0, right[c], right[c + 1])
            upper = jnp.where(lane == LANES - 1, left[c + 1], left[c])
            v = x[c + 1]
            lap = 2.0 * v - lower - upper
            out.append(
                2.0 * v - old[:, LANES * c : LANES * (c + 1)]
                - product[rows * c : rows * (c + 1)] - (DT2 * KAPPA) * lap
            )
        return jnp.concatenate(out, axis=1)

    group = 4

    def run(step, out, start, stop):
        whole = (stop - start) // group

        def one(g, carry):
            n = start + g * group
            out[:, lanes_at(n, group)] = stepped(step, n, group)
            return carry

        lax.fori_loop(0, whole, one, 0)
        n, count = start + whole * group, stop - start - whole * group
        if count:
            out[:, lanes_at(n, count)] = stepped(step, n, count)

    get_iface.wait()
    get_state.wait()
    get_older.wait()
    run(0, newer, itiles, tiles - 1)

    exchange(0, state[:, :iface])

    get_synth.wait()

    def synth_copy(n):
        to = {"grp": grp, "mer": mer, "sub": (sub + n) % nsub}
        if n == 0:
            to = {"grp": other, "mer": mer, "sub": sub}
        return pltpu.make_async_remote_copy(
            src_ref=synth_v.at[sub],
            dst_ref=synth_v.at[sub] if n else peer_v,
            send_sem=synth_send.at[n],
            recv_sem=synth_recv.at[n],
            device_id=to,
            device_id_type=MESH,
        )

    for k in [*ways, 0]:
        synth_copy(k).start()
    up[0].start()
    down[0].start()

    up[0].wait_recv()
    down[0].wait_recv()
    ahead = stepped(0, 0, itiles)
    base[...] = ahead
    ground[...] = dot(spread_out(synth_v[sub]), doubled(ahead))
    newer[:, pl.ds((tiles - 1) * LANES, LANES)] = stepped(0, tiles - 1, 1)
    up[1].start()

    for k in [*ways, 0]:
        synth_copy(k).wait_recv()
    high, low = halves(peer_v[...])
    high_all, low_all = halves(synth_v[...].reshape(nsub * rows, nsub * rows))
    product = dot(high, high_all) + (dot(high, low_all) + dot(low, high_all))
    operator[0] = spread_out(product * DT2)
    operator[1] = spread_out(peer_v[...])

    half = LANES // 2
    block = lax.broadcasted_iota(jnp.int32, (iface, domains), 0) // height
    spread = jnp.where(block == lax.broadcasted_iota(jnp.int32, (iface, domains), 1), 1.0, 0.0).astype(BF16)
    slot = lax.broadcasted_iota(jnp.int32, (iface, LANES), 1)
    slot = slot - lax.broadcasted_iota(jnp.int32, (iface, LANES), 0) % height

    def placed():
        names = first_in[:, pl.ds(height, 1), :].reshape(domains, LANES)
        names = dot(spread, names.astype(BF16))
        f = iota((iface, iface), 1)
        for n in range(2):
            name = jnp.sum(jnp.where(slot == n * height, names, 0.0), axis=1, keepdims=True)
            place[n * iface : (n + 1) * iface, :] = jnp.where(name == f, 1.0, 0.0).astype(BF16)

    def at_faces(step):
        all_of(step).wait_recv()
        if step == 0:
            placed()
        got = landed[step][:, pl.ds(0, height), :].reshape(iface, LANES).T
        high, low = halves(got)
        both = jnp.concatenate(
            [jnp.concatenate([v[:half], v[half:]], axis=1) for v in (high, low)], axis=0
        )
        out = dot(both, place[...])
        return out[:rows] + out[rows:]

    sums = doubled(at_faces(0))
    part[0] = (ground[...] + dot(operator[0], sums)).reshape(nsub, rows, iface)
    for k in ways:
        part_copy(0, k).start()
    part[1] = dot(operator[1], sums).reshape(nsub, rows, iface)
    exchange(1, summed(0))

    for k in ways:
        part_copy(1, k).start()
    run(1, final, itiles + 1, tiles - 1)
    newer[:, pl.ds(0, iface)] = base[...] + DT2 * summed(1)
    down[1].start()
    up[1].wait_recv()
    ahead = stepped(1, 0, itiles + 1)
    base[...] = ahead[:, :iface]
    final[:, pl.ds(iface, LANES)] = ahead[:, iface:]
    down[1].wait_recv()
    final[:, pl.ds((tiles - 1) * LANES, LANES)] = stepped(1, tiles - 1, 1)

    final[:, pl.ds(0, iface)] = base[...] + DT2 * at_faces(1)
    for step in range(ITERS):
        for k in ways:
            part_copy(step, k).wait_send()
        all_of(step).wait_send()
        up[step].wait_send()
        down[step].wait_send()
    for k in range(nsub):
        synth_copy(k).wait_send()

def written(final, newer, latest, prior, sem):
    step = final.shape[0] // CHUNKS
    copies = [
        pltpu.make_async_copy(
            src.at[pl.ds(c * step, step)], dst.at[0, pl.ds(c * step, step)], sem.at[n, c]
        )
        for c in range(CHUNKS)
        for n, (src, dst) in enumerate(((final, latest), (newer, prior)))
    ]
    for copy in copies:
        copy.start()
    for copy in copies:
        copy.wait()


CHUNKS = 1
ITERS = 2
DT2 = 0.5
KAPPA = 0.5
RESERVED = 64900000


def body(mesh_shape, field, previous, stiff, synth, owner, face, weight):
    domains, nsub = mesh_shape["mer"], mesh_shape["sub"]
    nz = 1 << (int(math.log2(domains)) // 2)
    ny = domains // nz
    _, rows, points = field.shape
    iface = owner.shape[1]
    height = iface // domains
    edge = stiff.shape[1]
    dma = pltpu.SemaphoreType.DMA
    anywhere = pl.BlockSpec(memory_space=pl.ANY)
    vmem = pl.BlockSpec(memory_space=pltpu.VMEM)
    scratch = [
        pltpu.VMEM((rows, points), F32),
        pltpu.VMEM((rows, points), F32),
        pltpu.VMEM((ITERS, 2, rows, LANES), F32),
        pltpu.VMEM((edge, edge), F32),
        pltpu.VMEM((nsub, rows, nsub * rows), F32),
        pltpu.VMEM((rows, nsub * rows), F32),
        pltpu.VMEM((1, iface), jnp.int32),
        pltpu.VMEM((1, iface), jnp.int32),
        pltpu.VMEM((1, iface), F32),
        pltpu.VMEM((ITERS, nsub, rows, iface), F32),
        pltpu.VMEM((ITERS, nsub - 1, rows, iface), F32),
        pltpu.VMEM((domains, height + 1, LANES), F32),
        pltpu.VMEM((domains, height + 1, LANES), F32),
        pltpu.VMEM((domains, height, LANES), F32),
        pltpu.VMEM((domains, height, LANES), F32),
        pltpu.VMEM((2 * edge, 2 * edge), BF16),
        pltpu.VMEM((2, nsub * rows, 4 * rows), BF16),
        pltpu.VMEM((2 * iface, iface), BF16),
        pltpu.VMEM((2 * iface, iface), BF16),
        pltpu.VMEM((rows, iface), F32),
        pltpu.VMEM((nsub * rows, iface), F32),
        dma((8,)),
        dma((ITERS, nsub - 1)),
        dma((ITERS, nsub - 1)),
        dma((ITERS,)),
        dma((ITERS,)),
        dma((ITERS, 2)),
        dma((ITERS, 2)),
        dma((nsub,)),
        dma((nsub,)),
    ]
    stepped = pl.pallas_call(
        functools.partial(kernel, ny, nz, nsub),
        out_shape=(pltpu.VMEM((rows, points), F32),) * 2,
        in_specs=[anywhere] * 7,
        out_specs=(vmem, vmem),
        scratch_shapes=scratch,
        compiler_params=pltpu.CompilerParams(
            collective_id=0, has_side_effects=True, vmem_limit_bytes=RESERVED
        ),
    )(
        field, previous, stiff, jnp.swapaxes(synth, 1, 2), owner.reshape(1, iface), face, weight
    )
    out = jax.ShapeDtypeStruct(field.shape, F32)
    return pl.pallas_call(
        written,
        out_shape=(out, out),
        in_specs=[anywhere] * 2,
        out_specs=(anywhere, anywhere),
        scratch_shapes=[dma((2, CHUNKS))],
        compiler_params=pltpu.CompilerParams(vmem_limit_bytes=1 << 20),
    )(*stepped)


def solution(mesh):
    in_specs = (
        P("grp", "sub", "mer"),
        P("grp", "sub", "mer"),
        P("grp", None, None),
        P("grp", None, "sub"),
        P("grp", "mer", None),
        P("grp", "mer"),
        P("grp", "mer"),
    )
    out_specs = (P("grp", "sub", "mer"), P("grp", "sub", "mer"))
    return jax.shard_map(
        functools.partial(body, dict(mesh.shape)),
        mesh=mesh,
        in_specs=in_specs,
        out_specs=out_specs,
        check_vma=False,
    )
```

```python
import functools
import math

import jax
import jax.numpy as jnp
from jax import lax
from jax.experimental import pallas as pl
from jax.experimental.pallas import tpu as pltpu
from jax.sharding import PartitionSpec as P

MESH = pl.DeviceIdType.MESH
F32, BF16 = jnp.float32, jnp.bfloat16
LANES = 128
NT = (((1,), (1,)), ((), ()))


def halves(value):
    high = value.astype(BF16)
    return high, (value - high.astype(F32)).astype(BF16)


def iota(shape, dim):
    return lax.broadcasted_iota(jnp.int32, shape, dim).astype(F32)


def lanes_at(n, count):
    start = n * LANES
    return pl.ds(start if isinstance(n, int) else pl.multiple_of(start, LANES), count * LANES)


def dot(a, b):
    return jnp.dot(a, b, preferred_element_type=F32)


def kernel(
    ny, nz, nsub, field, previous, stiff, synth_t, owner, face, weight, final, newer,
    state, older, halo, stiff_v, synth_v, peer_v, owner_v, face_v, weight_v,
    part, part_in, first, first_in, second, second_in,
    element, operator, pick, place, base, ground, sums,
    load_sem, part_send, part_recv, pack_send, pack_recv, halo_send, halo_recv, synth_send, synth_recv,
):
    rows, points = older.shape
    tiles = points // LANES
    domains, height, _ = second.shape
    iface = domains * height
    itiles = iface // LANES
    grp, mer, sub = lax.axis_index("grp"), lax.axis_index("mer"), lax.axis_index("sub")
    other = 1 - grp
    y, z = lax.div(mer, nz), lax.rem(mer, nz)
    above, below = lax.rem(mer + 1, domains), lax.rem(mer + domains - 1, domains)

    barrier = pltpu.get_barrier_semaphore()

    def greet(sem, **where):
        pl.semaphore_signal(sem, inc=1, device_id=where, device_id_type=MESH)

    offsets = [(a, b) for a in range(ny) for b in range(nz)]
    offsets.sort(key=lambda o: -(min(o[0], ny - o[0]) + min(o[1], nz - o[1])))
    y_at = [lax.rem(y + a, ny) * nz for a in range(ny)]
    z_at = [lax.rem(z + b, nz) for b in range(nz)]
    for a, b in offsets:
        greet(barrier, grp=other, mer=y_at[a] + z_at[b], sub=sub)
    for k in range(1, nsub):
        greet(barrier, grp=grp, mer=mer, sub=lax.rem(sub + k, nsub))
    greet(barrier, grp=grp, mer=above, sub=sub)
    greet(barrier, grp=grp, mer=below, sub=sub)

    def load(src, dst, n):
        copy = pltpu.make_async_copy(src, dst, load_sem.at[n])
        copy.start()
        return copy

    get_synth = load(synth_t.at[0], synth_v.at[sub], 0)
    get_iface = load(field.at[0, :, pl.ds(0, iface)], state.at[:, pl.ds(0, iface)], 1)
    get_owner = load(owner, owner_v, 2)
    get_face = load(face, face_v, 3)
    get_weight = load(weight, weight_v, 4)
    get_stiff = load(stiff.at[0], stiff_v, 5)
    get_state = load(
        field.at[0, :, pl.ds(iface, points - iface)], state.at[:, pl.ds(iface, points - iface)], 6
    )
    get_older = load(previous.at[0], older, 7)

    def spread_out(value):
        high, low = halves(value)
        high, low = high.astype(F32), low.astype(F32)
        return jnp.concatenate([high, high, low, low], axis=0).T.astype(BF16)

    def doubled(value):
        high, low = halves(value)
        return jnp.concatenate([high, low, high, low], axis=0)

    def part_copy(step, k):
        to = lax.rem(sub + k, nsub)
        return pltpu.make_async_remote_copy(
            src_ref=part.at[step, to],
            dst_ref=part_in.at[step, k - 1],
            send_sem=part_send.at[step, k - 1],
            recv_sem=part_recv.at[step, k - 1],
            device_id={"grp": grp, "mer": mer, "sub": to},
            device_id_type=MESH,
        )

    ways = sorted(range(1, nsub), key=lambda k: -min(k, nsub - k))

    def halo_copy(src, dst, to, step, way):
        return pltpu.make_async_remote_copy(
            src_ref=src,
            dst_ref=dst,
            send_sem=halo_send.at[step, way],
            recv_sem=halo_recv.at[step, way],
            device_id={"grp": grp, "mer": to, "sub": sub},
            device_id_type=MESH,
        )

    def lanes_of(ref, n):
        return ref.at[:, pl.ds(n * LANES, LANES)]

    up = [
        halo_copy(lanes_of(field.at[0], tiles - 1), halo.at[0, 0], above, 0, 0),
        halo_copy(lanes_of(newer, tiles - 1), halo.at[1, 0], above, 1, 0),
    ]
    down = [
        halo_copy(lanes_of(field.at[0], 0), halo.at[0, 1], below, 0, 1),
        halo_copy(lanes_of(newer, 0), halo.at[1, 1], below, 1, 1),
    ]
    get_owner.wait()
    get_face.wait()
    get_weight.wait()
    own = owner_v[...].astype(F32)
    across = jnp.broadcast_to(own, (iface, iface))
    i, j = iota((iface, iface), 0), iota((iface, iface), 1)
    down_own = jnp.sum(jnp.where(i == j, across, 0.0), axis=1, keepdims=True)
    rank = jnp.sum(jnp.where((down_own == across) & (i < j), 1.0, 0.0), axis=0, keepdims=True)
    late = (rank >= height).astype(F32)
    row = own * height + rank - height * late
    hit = jnp.where(i == row, 1.0, 0.0)
    pick[0:iface, :] = (hit * (1.0 - late)).astype(BF16)
    pick[iface:, :] = (hit * late).astype(BF16)
    left_half = lax.broadcasted_iota(jnp.int32, (iface, LANES), 1) < LANES // 2

    named = jnp.where(iota((LANES, iface), 0) == rank, face_v[...].astype(F32), 0.0).astype(BF16)
    chosen = jnp.where(iota((domains, iface), 0) == own, 1.0, 0.0).astype(BF16)
    names = lax.dot_general(chosen, named, NT, preferred_element_type=F32)
    first[:, pl.ds(height, 1), :] = names.reshape(domains, 1, LANES)

    sent, landed = (first, second), (first_in, second_in)

    def send_all(step):
        for a, b in offsets:
            to = y_at[a] + z_at[b]
            pltpu.make_async_remote_copy(
                src_ref=sent[step].at[to],
                dst_ref=landed[step].at[mer],
                send_sem=pack_send.at[step],
                recv_sem=pack_recv.at[step],
                device_id={"grp": other, "mer": to, "sub": sub},
                device_id_type=MESH,
            ).start()

    def all_of(step):
        return pltpu.make_async_remote_copy(
            src_ref=sent[step],
            dst_ref=landed[step],
            send_sem=pack_send.at[step],
            recv_sem=pack_recv.at[step],
            device_id={"grp": other, "mer": mer, "sub": sub},
            device_id_type=MESH,
        )

    def exchange(step, total):
        high, low = halves(total * weight_v[...])
        both = jnp.concatenate([high, low], axis=0)
        out = lax.dot_general(pick[...], both, NT, preferred_element_type=F32)
        out = out + pltpu.roll(out, LANES // 2, 1)
        out = jnp.where(left_half, out[:iface], out[iface:])
        sent[step][:, pl.ds(0, height), :] = out.reshape(domains, height, LANES)
        if step == 0:
            pl.semaphore_wait(barrier, domains + nsub - 1 + 2)
        send_all(step)

    def summed(n):
        total = part[n, sub]
        for k in ways[::-1]:
            part_copy(n, k).wait_recv()
            total = total + part_in[n, k - 1]
        return total

    get_stiff.wait()
    high, low = halves(stiff_v[...] * DT2)
    both = jnp.concatenate([high, low], axis=1)
    element[...] = jnp.concatenate([both, both], axis=0)
    lane = lax.broadcasted_iota(jnp.int32, (rows, LANES), 1)
    inner_low = jnp.where(mer > 0, 1.0, 0.0)
    inner_high = jnp.where(mer < domains - 1, 1.0, 0.0)

    def stepped(step, n, count):
        now, before = ((state, older), (newer, state))[step]
        static = isinstance(n, int)
        first, last = static and n == 0, static and n + count == tiles
        chunk = now[:, lanes_at(n if first else n - 1, count + 2 - first - last)]
        x = [chunk[:, LANES * c : LANES * (c + 1)] for c in range(chunk.shape[1] // LANES)]
        if first:
            x = [halo[step, 0] * inner_low] + x
        if last:
            x = x + [halo[step, 1] * inner_high]
        old = before[:, lanes_at(n, count)]
        high, low = halves(jnp.concatenate(x[1:-1], axis=0))
        product = dot(jnp.concatenate([high, low], axis=1), element[...])
        product = product[:, :LANES] + product[:, LANES:]
        right = [pltpu.roll(v, 1, 1) for v in x[:-1]]
        left = [pltpu.roll(v, LANES - 1, 1) for v in x[1:]]
        out = []
        for c in range(count):
            lower = jnp.where(lane == 0, right[c], right[c + 1])
            upper = jnp.where(lane == LANES - 1, left[c + 1], left[c])
            v = x[c + 1]
            lap = 2.0 * v - lower - upper
            out.append(
                2.0 * v - old[:, LANES * c : LANES * (c + 1)]
                - product[rows * c : rows * (c + 1)] - (DT2 * KAPPA) * lap
            )
        return jnp.concatenate(out, axis=1)

    group = 4

    def run(step, out, start, stop):
        whole = (stop - start) // group

        def one(g, carry):
            n = start + g * group
            out[:, lanes_at(n, group)] = stepped(step, n, group)
            return carry

        lax.fori_loop(0, whole, one, 0)
        n, count = start + whole * group, stop - start - whole * group
        if count:
            out[:, lanes_at(n, count)] = stepped(step, n, count)

    get_iface.wait()
    get_state.wait()
    get_older.wait()
    run(0, newer, itiles, tiles - 1)

    exchange(0, state[:, :iface])

    get_synth.wait()

    def synth_copy(n):
        to = {"grp": grp, "mer": mer, "sub": lax.rem(sub + n, nsub)}
        if n == 0:
            to = {"grp": other, "mer": mer, "sub": sub}
        return pltpu.make_async_remote_copy(
            src_ref=synth_v.at[sub],
            dst_ref=synth_v.at[sub] if n else peer_v,
            send_sem=synth_send.at[n],
            recv_sem=synth_recv.at[n],
            device_id=to,
            device_id_type=MESH,
        )

    for k in [*ways, 0]:
        synth_copy(k).start()
    up[0].start()
    down[0].start()

    up[0].wait_recv()
    down[0].wait_recv()
    ahead = stepped(0, 0, itiles)
    base[...] = ahead
    ground[...] = dot(spread_out(synth_v[sub]), doubled(ahead))
    newer[:, pl.ds((tiles - 1) * LANES, LANES)] = stepped(0, tiles - 1, 1)
    up[1].start()

    for k in [*ways, 0]:
        synth_copy(k).wait_recv()
    high, low = halves(peer_v[...])
    high_all, low_all = halves(synth_v[...].reshape(nsub * rows, nsub * rows))
    product = dot(high, high_all) + (dot(high, low_all) + dot(low, high_all))
    operator[0] = spread_out(product * DT2)
    operator[1] = spread_out(peer_v[...])

    half = LANES // 2
    block = lax.broadcasted_iota(jnp.int32, (iface, domains), 0) // height
    spread = jnp.where(block == lax.broadcasted_iota(jnp.int32, (iface, domains), 1), 1.0, 0.0).astype(BF16)
    slot = lax.broadcasted_iota(jnp.int32, (iface, LANES), 1)
    slot = slot - lax.broadcasted_iota(jnp.int32, (iface, LANES), 0) % height

    def placed():
        names = first_in[:, pl.ds(height, 1), :].reshape(domains, LANES)
        names = dot(spread, names.astype(BF16))
        f = iota((iface, iface), 1).astype(BF16)
        one, zero = jnp.ones((iface, iface), BF16), jnp.zeros((iface, iface), BF16)
        for n in range(2):
            name = jnp.sum(jnp.where(slot == n * height, names, 0.0), axis=1, keepdims=True)
            name = jnp.broadcast_to(name, (iface, iface)).astype(BF16)
            place[n * iface : (n + 1) * iface, :] = jnp.where(name == f, one, zero)

    def at_faces(step):
        all_of(step).wait_recv()
        if step == 0:
            placed()
        got = landed[step][:, pl.ds(0, height), :].reshape(iface, LANES).T
        high, low = halves(got)
        both = jnp.concatenate(
            [jnp.concatenate([v[:half], v[half:]], axis=1) for v in (high, low)], axis=0
        )
        out = dot(both, place[...])
        return out[:rows] + out[rows:]

    sums[...] = doubled(at_faces(0))
    part[0] = (ground[...] + dot(operator[0], sums[...])).reshape(nsub, rows, iface)
    for k in ways:
        part_copy(0, k).start()
    exchange(1, summed(0))

    part[1] = dot(operator[1], sums[...]).reshape(nsub, rows, iface)
    for k in ways:
        part_copy(1, k).start()
    run(1, final, itiles + 1, tiles - 1)
    newer[:, pl.ds(0, iface)] = base[...] + DT2 * summed(1)
    down[1].start()
    up[1].wait_recv()
    ahead = stepped(1, 0, itiles + 1)
    base[...] = ahead[:, :iface]
    final[:, pl.ds(iface, LANES)] = ahead[:, iface:]
    down[1].wait_recv()
    final[:, pl.ds((tiles - 1) * LANES, LANES)] = stepped(1, tiles - 1, 1)

    for step in range(ITERS):
        for k in ways:
            part_copy(step, k).wait_send()
        all_of(step).wait_send()
        up[step].wait_send()
        down[step].wait_send()
    for k in range(nsub):
        synth_copy(k).wait_send()
    final[:, pl.ds(0, iface)] = base[...] + DT2 * at_faces(1)


def written(final, newer, latest, prior, sem):
    step = final.shape[0] // CHUNKS
    copies = [
        pltpu.make_async_copy(
            src.at[pl.ds(c * step, step)], dst.at[0, pl.ds(c * step, step)], sem.at[n, c]
        )
        for c in range(CHUNKS)
        for n, (src, dst) in enumerate(((final, latest), (newer, prior)))
    ]
    for copy in copies:
        copy.start()
    for copy in copies:
        copy.wait()


CHUNKS = 1
ITERS = 2
DT2 = 0.5
KAPPA = 0.5
RESERVED = 64900000


def body(mesh_shape, field, previous, stiff, synth, owner, face, weight):
    domains, nsub = mesh_shape["mer"], mesh_shape["sub"]
    nz = 1 << (int(math.log2(domains)) // 2)
    ny = domains // nz
    _, rows, points = field.shape
    iface = owner.shape[1]
    height = iface // domains
    edge = stiff.shape[1]
    dma = pltpu.SemaphoreType.DMA
    anywhere = pl.BlockSpec(memory_space=pl.ANY)
    vmem = pl.BlockSpec(memory_space=pltpu.VMEM)
    scratch = [
        pltpu.VMEM((rows, points), F32),
        pltpu.VMEM((rows, points), F32),
        pltpu.VMEM((ITERS, 2, rows, LANES), F32),
        pltpu.VMEM((edge, edge), F32),
        pltpu.VMEM((nsub, rows, nsub * rows), F32),
        pltpu.VMEM((rows, nsub * rows), F32),
        pltpu.VMEM((1, iface), jnp.int32),
        pltpu.VMEM((1, iface), jnp.int32),
        pltpu.VMEM((1, iface), F32),
        pltpu.VMEM((ITERS, nsub, rows, iface), F32),
        pltpu.VMEM((ITERS, nsub - 1, rows, iface), F32),
        pltpu.VMEM((domains, height + 1, LANES), F32),
        pltpu.VMEM((domains, height + 1, LANES), F32),
        pltpu.VMEM((domains, height, LANES), F32),
        pltpu.VMEM((domains, height, LANES), F32),
        pltpu.VMEM((2 * edge, 2 * edge), BF16),
        pltpu.VMEM((2, nsub * rows, 4 * rows), BF16),
        pltpu.VMEM((2 * iface, iface), BF16),
        pltpu.VMEM((2 * iface, iface), BF16),
        pltpu.VMEM((rows, iface), F32),
        pltpu.VMEM((nsub * rows, iface), F32),
        pltpu.VMEM((4 * rows, iface), BF16),
        dma((8,)),
        dma((ITERS, nsub - 1)),
        dma((ITERS, nsub - 1)),
        dma((ITERS,)),
        dma((ITERS,)),
        dma((ITERS, 2)),
        dma((ITERS, 2)),
        dma((nsub,)),
        dma((nsub,)),
    ]
    stepped = pl.pallas_call(
        functools.partial(kernel, ny, nz, nsub),
        out_shape=(pltpu.VMEM((rows, points), F32),) * 2,
        in_specs=[anywhere] * 7,
        out_specs=(vmem, vmem),
        scratch_shapes=scratch,
        compiler_params=pltpu.CompilerParams(
            collective_id=0, has_side_effects=True, vmem_limit_bytes=RESERVED
        ),
    )(
        field, previous, stiff, jnp.swapaxes(synth, 1, 2), owner.reshape(1, iface), face, weight
    )
    out = jax.ShapeDtypeStruct(field.shape, F32)
    return pl.pallas_call(
        written,
        out_shape=(out, out),
        in_specs=[anywhere] * 2,
        out_specs=(anywhere, anywhere),
        scratch_shapes=[dma((2, CHUNKS))],
        compiler_params=pltpu.CompilerParams(vmem_limit_bytes=1 << 20),
    )(*stepped)


def solution(mesh):
    in_specs = (
        P("grp", "sub", "mer"),
        P("grp", "sub", "mer"),
        P("grp", None, None),
        P("grp", None, "sub"),
        P("grp", "mer", None),
        P("grp", "mer"),
        P("grp", "mer"),
    )
    out_specs = (P("grp", "sub", "mer"), P("grp", "sub", "mer"))
    return jax.shard_map(
        functools.partial(body, dict(mesh.shape)),
        mesh=mesh,
        in_specs=in_specs,
        out_specs=out_specs,
        check_vma=False,
    )
```

```python
import functools
import math

import jax
import jax.numpy as jnp
from jax import lax
from jax.experimental import pallas as pl
from jax.experimental.pallas import tpu as pltpu
from jax.sharding import PartitionSpec as P

MESH = pl.DeviceIdType.MESH
F32, BF16 = jnp.float32, jnp.bfloat16
LANES = 128
NT = (((1,), (1,)), ((), ()))


def halves(value):
    high = value.astype(BF16)
    return high, (value - high.astype(F32)).astype(BF16)


def iota(shape, dim):
    return lax.broadcasted_iota(jnp.int32, shape, dim).astype(F32)


def lanes_at(n, count):
    start = n * LANES
    return pl.ds(start if isinstance(n, int) else pl.multiple_of(start, LANES), count * LANES)


def dot(a, b):
    return jnp.dot(a, b, preferred_element_type=F32)


def kernel(
    ny, nz, nsub, field, previous, stiff, synth_t, owner, face, weight, final, newer,
    state, older, halo, stiff_v, synth_v, peer_v, owner_v, face_v, weight_v,
    part, part_in, first, first_in, second, second_in,
    element, operator, pick, place, base, ground, sums,
    load_sem, part_send, part_recv, pack_send, pack_recv, halo_send, halo_recv, synth_send, synth_recv,
):
    rows, points = older.shape
    tiles = points // LANES
    domains, height, _ = second.shape
    iface = domains * height
    itiles = iface // LANES
    grp, mer, sub = lax.axis_index("grp"), lax.axis_index("mer"), lax.axis_index("sub")
    other = 1 - grp
    y, z = lax.div(mer, nz), lax.rem(mer, nz)
    above, below = lax.rem(mer + 1, domains), lax.rem(mer + domains - 1, domains)

    barrier = pltpu.get_barrier_semaphore()

    def greet(sem, **where):
        pl.semaphore_signal(sem, inc=1, device_id=where, device_id_type=MESH)

    offsets = [(a, b) for a in range(ny) for b in range(nz)]
    offsets.sort(key=lambda o: -(min(o[0], ny - o[0]) + min(o[1], nz - o[1])))
    y_at = [lax.rem(y + a, ny) * nz for a in range(ny)]
    z_at = [lax.rem(z + b, nz) for b in range(nz)]
    for a, b in offsets:
        greet(barrier, grp=other, mer=y_at[a] + z_at[b], sub=sub)
    for k in range(1, nsub):
        greet(barrier, grp=grp, mer=mer, sub=lax.rem(sub + k, nsub))
    greet(barrier, grp=grp, mer=above, sub=sub)
    greet(barrier, grp=grp, mer=below, sub=sub)

    def load(src, dst, n):
        copy = pltpu.make_async_copy(src, dst, load_sem.at[n])
        copy.start()
        return copy

    get_synth = load(synth_t.at[0], synth_v.at[sub], 0)
    get_iface = load(field.at[0, :, pl.ds(0, iface)], state.at[:, pl.ds(0, iface)], 1)
    get_owner = load(owner, owner_v, 2)
    get_face = load(face, face_v, 3)
    get_weight = load(weight, weight_v, 4)
    get_stiff = load(stiff.at[0], stiff_v, 5)
    get_state = load(
        field.at[0, :, pl.ds(iface, points - iface)], state.at[:, pl.ds(iface, points - iface)], 6
    )
    get_older = load(previous.at[0], older, 7)

    def spread_out(value):
        high, low = halves(value)
        high, low = high.astype(F32), low.astype(F32)
        return jnp.concatenate([high, high, low, low], axis=0).T.astype(BF16)

    def doubled(value):
        high, low = halves(value)
        return jnp.concatenate([high, low, high, low], axis=0)

    def part_copy(step, k):
        to = lax.rem(sub + k, nsub)
        return pltpu.make_async_remote_copy(
            src_ref=part.at[step, to],
            dst_ref=part_in.at[step, k - 1],
            send_sem=part_send.at[step, k - 1],
            recv_sem=part_recv.at[step, k - 1],
            device_id={"grp": grp, "mer": mer, "sub": to},
            device_id_type=MESH,
        )

    ways = sorted(range(1, nsub), key=lambda k: -min(k, nsub - k))

    def halo_copy(src, dst, to, step, way):
        return pltpu.make_async_remote_copy(
            src_ref=src,
            dst_ref=dst,
            send_sem=halo_send.at[step, way],
            recv_sem=halo_recv.at[step, way],
            device_id={"grp": grp, "mer": to, "sub": sub},
            device_id_type=MESH,
        )

    def lanes_of(ref, n):
        return ref.at[:, pl.ds(n * LANES, LANES)]

    up = [
        halo_copy(lanes_of(field.at[0], tiles - 1), halo.at[0, 0], above, 0, 0),
        halo_copy(lanes_of(newer, tiles - 1), halo.at[1, 0], above, 1, 0),
    ]
    down = [
        halo_copy(lanes_of(field.at[0], 0), halo.at[0, 1], below, 0, 1),
        halo_copy(lanes_of(newer, 0), halo.at[1, 1], below, 1, 1),
    ]
    get_owner.wait()
    get_face.wait()
    get_weight.wait()
    own = owner_v[...].astype(F32)
    across = jnp.broadcast_to(own, (iface, iface))
    i, j = iota((iface, iface), 0), iota((iface, iface), 1)
    down_own = jnp.sum(jnp.where(i == j, across, 0.0), axis=1, keepdims=True)
    rank = jnp.sum(jnp.where((down_own == across) & (i < j), 1.0, 0.0), axis=0, keepdims=True)
    late = (rank >= height).astype(F32)
    row = own * height + rank - height * late
    hit = jnp.where(i == row, 1.0, 0.0)
    picked = jnp.concatenate([(hit * (1.0 - late)).astype(BF16), (hit * late).astype(BF16)], axis=1)
    pick[...] = jnp.concatenate([picked, picked], axis=1)

    named = jnp.where(iota((LANES, iface), 0) == rank, face_v[...].astype(F32), 0.0).astype(BF16)
    chosen = jnp.where(iota((domains, iface), 0) == own, 1.0, 0.0).astype(BF16)
    names = lax.dot_general(chosen, named, NT, preferred_element_type=F32)
    first[:, pl.ds(height, 1), :] = names.reshape(domains, 1, LANES)

    sent, landed = (first, second), (first_in, second_in)

    def send_all(step):
        for a, b in offsets:
            to = y_at[a] + z_at[b]
            pltpu.make_async_remote_copy(
                src_ref=sent[step].at[to],
                dst_ref=landed[step].at[mer],
                send_sem=pack_send.at[step],
                recv_sem=pack_recv.at[step],
                device_id={"grp": other, "mer": to, "sub": sub},
                device_id_type=MESH,
            ).start()

    def all_of(step):
        return pltpu.make_async_remote_copy(
            src_ref=sent[step],
            dst_ref=landed[step],
            send_sem=pack_send.at[step],
            recv_sem=pack_recv.at[step],
            device_id={"grp": other, "mer": mer, "sub": sub},
            device_id_type=MESH,
        )

    def exchange(step, total):
        high, low = halves(total * weight_v[...])
        none = jnp.zeros_like(high)
        both = jnp.concatenate(
            [
                jnp.concatenate([high, none, low, none], axis=1),
                jnp.concatenate([none, high, none, low], axis=1),
            ],
            axis=0,
        )
        out = lax.dot_general(pick[...], both, NT, preferred_element_type=F32)
        sent[step][:, pl.ds(0, height), :] = out.reshape(domains, height, LANES)
        if step == 0:
            pl.semaphore_wait(barrier, domains + nsub - 1 + 2)
        send_all(step)

    def summed(n):
        total = part[n, sub]
        for k in ways[::-1]:
            part_copy(n, k).wait_recv()
            total = total + part_in[n, k - 1]
        return total

    get_stiff.wait()
    high, low = halves(stiff_v[...] * DT2)
    both = jnp.concatenate([high, low], axis=1)
    element[...] = jnp.concatenate([both, both], axis=0)
    lane = lax.broadcasted_iota(jnp.int32, (rows, LANES), 1)
    inner_low = jnp.where(mer > 0, 1.0, 0.0)
    inner_high = jnp.where(mer < domains - 1, 1.0, 0.0)

    def stepped(step, n, count):
        now, before = ((state, older), (newer, state))[step]
        static = isinstance(n, int)
        first, last = static and n == 0, static and n + count == tiles
        chunk = now[:, lanes_at(n if first else n - 1, count + 2 - first - last)]
        x = [chunk[:, LANES * c : LANES * (c + 1)] for c in range(chunk.shape[1] // LANES)]
        if first:
            x = [halo[step, 0] * inner_low] + x
        if last:
            x = x + [halo[step, 1] * inner_high]
        old = before[:, lanes_at(n, count)]
        high, low = halves(jnp.concatenate(x[1:-1], axis=0))
        product = dot(jnp.concatenate([high, low], axis=1), element[...])
        product = product[:, :LANES] + product[:, LANES:]
        right = [pltpu.roll(v, 1, 1) for v in x[:-1]]
        left = [pltpu.roll(v, LANES - 1, 1) for v in x[1:]]
        out = []
        for c in range(count):
            lower = jnp.where(lane == 0, right[c], right[c + 1])
            upper = jnp.where(lane == LANES - 1, left[c + 1], left[c])
            v = x[c + 1]
            lap = 2.0 * v - lower - upper
            out.append(
                2.0 * v - old[:, LANES * c : LANES * (c + 1)]
                - product[rows * c : rows * (c + 1)] - (DT2 * KAPPA) * lap
            )
        return jnp.concatenate(out, axis=1)

    group = 4

    def run(step, out, start, stop):
        whole = (stop - start) // group

        def one(g, carry):
            n = start + g * group
            out[:, lanes_at(n, group)] = stepped(step, n, group)
            return carry

        lax.fori_loop(0, whole, one, 0)
        n, count = start + whole * group, stop - start - whole * group
        if count:
            out[:, lanes_at(n, count)] = stepped(step, n, count)

    get_iface.wait()
    get_state.wait()
    get_older.wait()
    run(0, newer, itiles, tiles - 1)

    exchange(0, state[:, :iface])

    get_synth.wait()

    def synth_copy(n):
        to = {"grp": grp, "mer": mer, "sub": lax.rem(sub + n, nsub)}
        if n == 0:
            to = {"grp": other, "mer": mer, "sub": sub}
        return pltpu.make_async_remote_copy(
            src_ref=synth_v.at[sub],
            dst_ref=synth_v.at[sub] if n else peer_v,
            send_sem=synth_send.at[n],
            recv_sem=synth_recv.at[n],
            device_id=to,
            device_id_type=MESH,
        )

    for k in [*ways, 0]:
        synth_copy(k).start()
    up[0].start()
    down[0].start()

    up[0].wait_recv()
    down[0].wait_recv()
    ahead = stepped(0, 0, itiles)
    base[...] = ahead
    ground[...] = dot(spread_out(synth_v[sub]), doubled(ahead))
    newer[:, pl.ds((tiles - 1) * LANES, LANES)] = stepped(0, tiles - 1, 1)
    up[1].start()

    for k in [*ways, 0]:
        synth_copy(k).wait_recv()
    high, low = halves(peer_v[...])
    high_all, low_all = halves(synth_v[...].reshape(nsub * rows, nsub * rows))
    product = dot(high, high_all) + (dot(high, low_all) + dot(low, high_all))
    operator[0] = spread_out(product * DT2)
    operator[1] = spread_out(peer_v[...])

    half = LANES // 2
    block = lax.broadcasted_iota(jnp.int32, (iface, domains), 0) // height
    spread = jnp.where(block == lax.broadcasted_iota(jnp.int32, (iface, domains), 1), 1.0, 0.0).astype(BF16)
    slot = lax.broadcasted_iota(jnp.int32, (iface, LANES), 1)
    slot = slot - lax.broadcasted_iota(jnp.int32, (iface, LANES), 0) % height

    def placed():
        names = first_in[:, pl.ds(height, 1), :].reshape(domains, LANES)
        names = dot(spread, names.astype(BF16))
        f = iota((iface, iface), 1).astype(BF16)
        one, zero = jnp.ones((iface, iface), BF16), jnp.zeros((iface, iface), BF16)
        for n in range(2):
            name = jnp.sum(jnp.where(slot == n * height, names, 0.0), axis=1, keepdims=True)
            name = jnp.broadcast_to(name, (iface, iface)).astype(BF16)
            place[n * iface : (n + 1) * iface, :] = jnp.where(name == f, one, zero)

    def at_faces(step):
        all_of(step).wait_recv()
        if step == 0:
            placed()
        got = landed[step][:, pl.ds(0, height), :].reshape(iface, LANES).T
        high, low = halves(got)
        both = jnp.concatenate(
            [jnp.concatenate([v[:half], v[half:]], axis=1) for v in (high, low)], axis=0
        )
        out = dot(both, place[...])
        return out[:rows] + out[rows:]

    sums[...] = doubled(at_faces(0))
    part[0] = (ground[...] + dot(operator[0], sums[...])).reshape(nsub, rows, iface)
    for k in ways:
        part_copy(0, k).start()
    exchange(1, summed(0))

    part[1] = dot(operator[1], sums[...]).reshape(nsub, rows, iface)
    for k in ways:
        part_copy(1, k).start()
    run(1, final, itiles + 1, tiles - 1)
    newer[:, pl.ds(0, iface)] = base[...] + DT2 * summed(1)
    down[1].start()
    up[1].wait_recv()
    ahead = stepped(1, 0, itiles + 1)
    base[...] = ahead[:, :iface]
    final[:, pl.ds(iface, LANES)] = ahead[:, iface:]
    down[1].wait_recv()
    final[:, pl.ds((tiles - 1) * LANES, LANES)] = stepped(1, tiles - 1, 1)

    for step in range(ITERS):
        for k in ways:
            part_copy(step, k).wait_send()
        all_of(step).wait_send()
        up[step].wait_send()
        down[step].wait_send()
    for k in range(nsub):
        synth_copy(k).wait_send()
    final[:, pl.ds(0, iface)] = base[...] + DT2 * at_faces(1)


def written(final, newer, latest, prior, sem):
    step = final.shape[0] // CHUNKS
    copies = [
        pltpu.make_async_copy(
            src.at[pl.ds(c * step, step)], dst.at[0, pl.ds(c * step, step)], sem.at[n, c]
        )
        for c in range(CHUNKS)
        for n, (src, dst) in enumerate(((final, latest), (newer, prior)))
    ]
    for copy in copies:
        copy.start()
    for copy in copies:
        copy.wait()


CHUNKS = 1
ITERS = 2
DT2 = 0.5
KAPPA = 0.5
RESERVED = 64900000


def body(mesh_shape, field, previous, stiff, synth, owner, face, weight):
    domains, nsub = mesh_shape["mer"], mesh_shape["sub"]
    nz = 1 << (int(math.log2(domains)) // 2)
    ny = domains // nz
    _, rows, points = field.shape
    iface = owner.shape[1]
    height = iface // domains
    edge = stiff.shape[1]
    dma = pltpu.SemaphoreType.DMA
    anywhere = pl.BlockSpec(memory_space=pl.ANY)
    vmem = pl.BlockSpec(memory_space=pltpu.VMEM)
    scratch = [
        pltpu.VMEM((rows, points), F32),
        pltpu.VMEM((rows, points), F32),
        pltpu.VMEM((ITERS, 2, rows, LANES), F32),
        pltpu.VMEM((edge, edge), F32),
        pltpu.VMEM((nsub, rows, nsub * rows), F32),
        pltpu.VMEM((rows, nsub * rows), F32),
        pltpu.VMEM((1, iface), jnp.int32),
        pltpu.VMEM((1, iface), jnp.int32),
        pltpu.VMEM((1, iface), F32),
        pltpu.VMEM((ITERS, nsub, rows, iface), F32),
        pltpu.VMEM((ITERS, nsub - 1, rows, iface), F32),
        pltpu.VMEM((domains, height + 1, LANES), F32),
        pltpu.VMEM((domains, height + 1, LANES), F32),
        pltpu.VMEM((domains, height, LANES), F32),
        pltpu.VMEM((domains, height, LANES), F32),
        pltpu.VMEM((2 * edge, 2 * edge), BF16),
        pltpu.VMEM((2, nsub * rows, 4 * rows), BF16),
        pltpu.VMEM((iface, 4 * iface), BF16),
        pltpu.VMEM((2 * iface, iface), BF16),
        pltpu.VMEM((rows, iface), F32),
        pltpu.VMEM((nsub * rows, iface), F32),
        pltpu.VMEM((4 * rows, iface), BF16),
        dma((8,)),
        dma((ITERS, nsub - 1)),
        dma((ITERS, nsub - 1)),
        dma((ITERS,)),
        dma((ITERS,)),
        dma((ITERS, 2)),
        dma((ITERS, 2)),
        dma((nsub,)),
        dma((nsub,)),
    ]
    stepped = pl.pallas_call(
        functools.partial(kernel, ny, nz, nsub),
        out_shape=(pltpu.VMEM((rows, points), F32),) * 2,
        in_specs=[anywhere] * 7,
        out_specs=(vmem, vmem),
        scratch_shapes=scratch,
        compiler_params=pltpu.CompilerParams(
            collective_id=0, has_side_effects=True, vmem_limit_bytes=RESERVED
        ),
    )(
        field, previous, stiff, jnp.swapaxes(synth, 1, 2), owner.reshape(1, iface), face, weight
    )
    out = jax.ShapeDtypeStruct(field.shape, F32)
    return pl.pallas_call(
        written,
        out_shape=(out, out),
        in_specs=[anywhere] * 2,
        out_specs=(anywhere, anywhere),
        scratch_shapes=[dma((2, CHUNKS))],
        compiler_params=pltpu.CompilerParams(vmem_limit_bytes=1 << 20),
    )(*stepped)


def solution(mesh):
    in_specs = (
        P("grp", "sub", "mer"),
        P("grp", "sub", "mer"),
        P("grp", None, None),
        P("grp", None, "sub"),
        P("grp", "mer", None),
        P("grp", "mer"),
        P("grp", "mer"),
    )
    out_specs = (P("grp", "sub", "mer"), P("grp", "sub", "mer"))
    return jax.shard_map(
        functools.partial(body, dict(mesh.shape)),
        mesh=mesh,
        in_specs=in_specs,
        out_specs=out_specs,
        check_vma=False,
    )
```
